256 devices in a mesh: kv: 4 (over y), blk: 64 (over z, x, core).
Axes of the slice: x: 4, y: 4, z: 8, core: 2. Of those that a mesh axis runs over, the one named last changes fastest.
Arguments:
- queries: bfloat16 [64, 2560], P('blk', 'kv'), may hold values from -104 to 104
- kv_pool: bfloat16 [8192, 2, 64, 512], P('blk', None, None, 'kv'), may hold values from -4 to 4
- block_table: int32 [64, 256], replicated, may hold values from -1 to 8191, as said below
- lengths: int32 [64], replicated, may hold values from 2 to 16384, as said below
- residual: bfloat16 [64, 2560], P('blk', 'kv'), may hold values from -6 to 6
- out_weight: bfloat16 [2560, 2560], P('kv'), may hold values from -0.125 to 0.125
- norm_gain: bfloat16 [2560], replicated, may hold values from 0.5 to 1.5
- qkv_weight: bfloat16 [2560, 3584], P(None, 'kv'), may hold values from -0.125 to 0.125
Outputs:
- stream_out: bfloat16 [64, 2560], P('blk', 'kv')
- next_qkv: bfloat16 [64, 3584], P('blk', 'kv')
The draws below stay inside these ranges and needn't reach their ends.
Inputs may be any that keep to these rules, and one draw needn't show every extreme that they name: `block_table`: row r names ceil(lengths[r] / 64) pool blocks, then -1; different rows and slots name different blocks. `lengths`: some request has exactly 16384 tokens.
All inputs are finite; a program needn't handle non-finite values.
Results may differ from the reference program's by a relative error of at most 0.0065.
Values may be sent and summed in bfloat16 or wider, within the bound.
A program may use at most 64 MiB of HBM per device.

```python
import jax
import jax.numpy as jnp
from jax import lax

D = 2560
HEADS = 20
KVH = 4
HEAD = 128
BLOCK = 64
REQ_DEV = 1
MAXB = 256
NB_DEV = 128
NBLK = 8192
REQ = 64
GROUP = 5
QKV = 3584


def layout(key):
    base = jax.random.fold_in(key, 7)
    key_a, key_b, key_c, key_d = jax.random.split(base, 4)
    half = REQ // 2
    first = jax.random.randint(key_a, (half,), 1, MAXB - 1)
    counts = jnp.stack([first, MAXB - 1 - first], axis=1).reshape(REQ)
    counts = counts.at[0].set(MAXB).at[1].set(1)
    order = jax.random.permutation(key_b, REQ)
    counts = counts[order]
    tail = jax.random.randint(key_c, (REQ,), 2, BLOCK + 1)
    tail = jnp.where(counts == MAXB, BLOCK, tail)
    lengths = (counts - 1) * BLOCK + tail
    holders = NBLK // NB_DEV
    request = jnp.arange(REQ, dtype=jnp.int32)
    home = request // REQ_DEV
    before = (home + holders - 1) % holders
    first_block = before * NB_DEV + request % REQ_DEV
    position = jnp.arange(NBLK, dtype=jnp.int32)
    reserved = position % NB_DEV < REQ_DEV
    scores = jax.random.permutation(key_d, NBLK).astype(jnp.int32) + jnp.where(reserved, NBLK, 0).astype(jnp.int32)
    rest = jnp.argsort(scores).astype(jnp.int32)
    extra = counts - 1
    starts = jnp.cumsum(extra) - extra
    slot = jnp.arange(MAXB, dtype=jnp.int32)
    index = jnp.clip(starts[:, None] + slot[None, :] - 1, 0, NBLK - 1)
    later = jnp.where(slot[None, :] < counts[:, None], rest[index], -1)
    table = jnp.where(slot[None, :] == 0, first_block[:, None], later)
    return (table.astype(jnp.int32), lengths.astype(jnp.int32))


def pool_block(key, block):
    block_key = jax.random.fold_in(jax.random.fold_in(key, 11), block)
    key_k, key_v = jax.random.split(block_key)
    keys = jnp.clip(jax.random.normal(key_k, (BLOCK, KVH * HEAD), jnp.float32), -4.0, 4.0)
    values = jnp.clip(jax.random.normal(key_v, (BLOCK, KVH * HEAD), jnp.float32), -4.0, 4.0)
    return jnp.stack([keys, values])


def draw_kv_pool(key, part):
    return lax.map(lambda block: pool_block(key, block).astype(jnp.bfloat16), jnp.arange(NBLK))


def draw_block_table(key, part):
    return layout(key)[0]


def draw_lengths(key, part):
    return layout(key)[1]


def draw_queries(key, part):
    query_key = jax.random.fold_in(key, 13)
    request = jnp.arange(REQ, dtype=jnp.int32)
    sharp = request % 8 == 5
    spread = jnp.where(sharp, jnp.float32(16.0), jnp.float32(1.5))
    result = spread[:, None] * jnp.clip(jax.random.normal(query_key, (REQ, HEADS * HEAD), jnp.float32), -6.0, 6.0)
    return result.astype(jnp.bfloat16)


def level_of(rng, dims, pieces, least, largest):
    loudness = 1.0
    for axis_at, parts in pieces:
        steps = jax.random.uniform(jax.random.fold_in(jax.random.fold_in(rng, 6), axis_at), (parts,), jnp.float32, least / len(pieces), largest / len(pieces))
        loudness = loudness * jnp.repeat(jnp.exp(steps), dims[axis_at] // parts).reshape((-1,) + (1,) * (len(dims) - 1 - axis_at))
    return loudness


def centred(stream_key, extent, width, most, pieces=(), held_as=jnp.bfloat16):
    gain = level_of(stream_key, extent, pieces, -0.22, 0.18) if pieces else 1.0
    values = jax.random.normal(stream_key, extent, jnp.float32) * width * gain
    return jnp.minimum(jnp.maximum(values, -most), most).astype(held_as)


def setup_inputs(seed: int = 0) -> dict:
    key_list = jax.random.split(jax.random.key(seed), 9)
    return {
        "queries": draw_queries(jax.random.fold_in(key_list[8], 71), 0),
        "kv_pool": draw_kv_pool(jax.random.fold_in(key_list[8], 71), 0),
        "block_table": draw_block_table(jax.random.fold_in(key_list[8], 71), 0),
        "lengths": draw_lengths(jax.random.fold_in(key_list[8], 71), 0),
        "residual": centred(key_list[4], (REQ, D), 1.0, 6.0, ((0, 64), (1, 4))),
        "out_weight": centred(key_list[5], (D, D), D ** -0.5, 0.125, ((0, 4),)),
        "norm_gain": jnp.clip(1.0 + 0.1 * jax.random.normal(key_list[6], (D,), jnp.float32), 0.5, 1.5).astype(jnp.bfloat16),
        "qkv_weight": centred(key_list[7], (D, QKV), D ** -0.5, 0.125, ((1, 4),)),
    }


def attend_one(args, kv_pool):
    query, row, length = args
    blocks = kv_pool[jnp.maximum(row, 0)]
    keys = blocks[:, 0].reshape(MAXB, BLOCK, KVH, HEAD).astype(jnp.float32)
    values = blocks[:, 1].reshape(MAXB, BLOCK, KVH, HEAD).astype(jnp.float32)
    heads = query.reshape(KVH, GROUP, HEAD).astype(jnp.float32)
    score = jnp.einsum('btgd,ghd->bgth', keys, heads) * HEAD ** (-0.5)
    position = jnp.arange(MAXB)[:, None] * BLOCK + jnp.arange(BLOCK)[None, :]
    valid = (position < length) & (row[:, None] >= 0)
    mask = valid[:, None, :, None]
    score = jnp.where(mask, score, jnp.float32(-1e+30))
    block_max = lax.optimization_barrier(jnp.max(score, axis=2))
    expo = jnp.exp(score - block_max[:, :, None, :]) * mask.astype(jnp.float32)
    block_sum = lax.optimization_barrier(jnp.sum(expo, axis=2))
    rounded = expo.astype(jnp.bfloat16).astype(jnp.float32)
    block_out = jnp.einsum('bgth,btgd->bghd', rounded, values)
    top = lax.optimization_barrier(jnp.max(block_max, axis=0))
    scale = jnp.exp(block_max - top[None])
    total = lax.optimization_barrier(jnp.sum(scale * block_sum, axis=0))
    out = lax.optimization_barrier(jnp.sum(scale[..., None] * block_out, axis=0)) / total[..., None]
    return out.reshape(HEADS * HEAD)

def reference(queries, kv_pool, block_table, lengths, residual, out_weight, norm_gain, qkv_weight):
    attn = lax.map(lambda args: attend_one(args, kv_pool), (queries, block_table, lengths))
    attn = attn.astype(jnp.bfloat16)
    hidden = residual.astype(jnp.float32) + jnp.dot(attn, out_weight, preferred_element_type=jnp.float32)
    stream_out = hidden.astype(jnp.bfloat16)
    inverse = lax.rsqrt(lax.optimization_barrier(jnp.mean(hidden * hidden, axis=1, keepdims=True)) + 1e-05)
    normed = (hidden * inverse * norm_gain.astype(jnp.float32)[None, :]).astype(jnp.bfloat16)
    next_qkv = jnp.dot(normed, qkv_weight, preferred_element_type=jnp.float32).astype(jnp.bfloat16)
    return (stream_out, next_qkv)
```

```python
import functools

import jax
import jax.numpy as jnp
from jax import lax
from jax.experimental import pallas as pl
from jax.experimental.pallas import tpu as pltpu
from jax.sharding import PartitionSpec as P

HEAD = 128
MESH = pl.DeviceIdType.MESH
F32 = jnp.float32
BF16 = jnp.bfloat16
NEG = -1e30


def rows_of(x, count, width):
    rows = [x[:, i * width : (i + 1) * width] for i in range(count)]
    rows.append(jnp.zeros((8 - count, width), x.dtype))
    return jnp.concatenate(rows, axis=0)


def split(x):
    hi = x.astype(BF16)
    return hi, (x - hi.astype(F32)).astype(BF16)


def dot(a, b):
    return jnp.dot(a, b, preferred_element_type=F32)


def kernel(
    num_blk, num_kv, group,
    q_hbm, kv_hbm, table_hbm, len_hbm, res_hbm, wo_hbm, gain_hbm, wq_hbm,
    stream_ref, next_ref,
    q_v, kv_v, table_v, len_s, res_v, wo_v, gain_v, wq_v,
    qsend, qall, code_v, expand, count8, qblk, outs, msgf, msg, recv, recvf, hbuf, hsum,
    local_sem, qs_sem, qr_sem, ms_sem, mr_sem, hs_sem, hr_sem,
):
    me = lax.axis_index("blk")
    kv = lax.axis_index("kv")
    num_req = qall.shape[0]
    blocks = kv_v.shape[0]
    block = kv_v.shape[2]
    width = hsum.shape[1]
    cols = res_v.shape[1]

    pairs = [
        (q_hbm, q_v), (table_hbm, table_v), (len_hbm, len_s), (kv_hbm, kv_v),
        (res_hbm, res_v), (gain_hbm, gain_v), (wo_hbm, wo_v), (wq_hbm, wq_v),
    ]
    loads = [pltpu.make_async_copy(a, b, local_sem.at[i]) for i, (a, b) in enumerate(pairs)]

    def peer_of(j):
        step = num_blk // 2 + (1 - 2 * (j % 2)) * ((j + 1) // 2)
        return lax.rem(me + step, num_blk)

    barrier = pltpu.get_barrier_semaphore()
    loads[0].start()
    loads[1].start()
    loads[2].start()

    def greet(j, carry):
        pl.semaphore_signal(barrier, inc=1, device_id={"blk": peer_of(j)}, device_id_type=MESH)
        return carry

    lax.fori_loop(0, num_blk - 1, greet, 0)
    for j in range(1, num_kv):
        pl.semaphore_signal(
            barrier, inc=1, device_id={"kv": lax.rem(kv + j, num_kv)}, device_id_type=MESH
        )
    for load in loads[3:]:
        load.start()

    loads[0].wait()
    mine = rows_of(q_v[...].astype(F32), group, HEAD).astype(BF16)
    qsend[...] = mine
    qall[me] = mine

    loads[1].wait()
    loads[2].wait()
    max_blocks = table_v.shape[1]
    lane = lax.broadcasted_iota(jnp.int32, (1, 128), 1)
    row_id = lax.broadcasted_iota(jnp.int32, (blocks, 128), 0)
    best = jnp.full((blocks, 128), -1.0, F32)
    first = me * blocks
    for part in range(max_blocks // 128):
        at = lane + part * 128

        def match(i, acc):
            local = table_v[pl.ds(pl.multiple_of(i * 8, 8), 8), part * 128 : (part + 1) * 128] - first
            for c in range(8):
                r = i * 8 + c
                tokens = jnp.clip(len_s[r] - at * block, 0, block)
                code = (tokens + r * 128).astype(F32)
                acc = jnp.where(row_id == local[c : c + 1, :], code, acc)
            return acc

        best = lax.fori_loop(0, num_req // 8, match, best)
    code = jnp.broadcast_to(jnp.max(best, axis=1, keepdims=True), (blocks, 128))
    code_v[...] = code
    code_row = jnp.transpose(code)[:num_req, :].astype(jnp.int32)
    owns = (code_row >> 7) == lax.broadcasted_iota(jnp.int32, (num_req, blocks), 0)

    column = lax.broadcasted_iota(jnp.int32, (16, num_req * 8), 1)
    sub = lax.broadcasted_iota(jnp.int32, (16, 128), 0)

    def widen(i, carry):
        a = jnp.broadcast_to(code_v[pl.ds(2 * i, 1), :], (16, 128))
        b = jnp.broadcast_to(code_v[pl.ds(2 * i + 1, 1), :], (16, 128))
        both = jnp.where(sub < 8, a, b).astype(jnp.int32)
        target = (both >> 7) * 8 + (sub & 7)
        wide = jnp.concatenate([target] * (num_req * 8 // 128), axis=1)
        at16 = pl.multiple_of(i * 16, 16)
        expand[pl.ds(at16, 16), :] = jnp.where(column == wide, 1.0, 0.0).astype(BF16)
        count8[pl.ds(at16, 16), :] = jnp.where(both >= 0, both & 127, 0)
        return carry

    lax.fori_loop(0, blocks // 2, widen, 0, unroll=4)

    pl.semaphore_wait(barrier, num_blk - 1 + num_kv - 1)

    def send_query(j, carry):
        pltpu.make_async_remote_copy(
            src_ref=qsend, dst_ref=qall.at[me], send_sem=qs_sem, recv_sem=qr_sem,
            device_id={"blk": peer_of(j)}, device_id_type=MESH,
        ).start()
        return carry

    lax.fori_loop(0, num_blk - 1, send_query, 0)
    loads[3].wait()
    others = pl.ds(0, num_blk - 1)
    pltpu.make_async_copy(qall.at[others], qall.at[others], qr_sem).wait()

    flat = qall[...].astype(F32).reshape(num_req * 8, HEAD).astype(BF16)
    qblk[...] = dot(expand[...], flat).astype(BF16)

    rows = 32
    toks = 4 * block
    r_i = lax.broadcasted_iota(jnp.int32, (rows, toks), 0) // 8
    t_i = lax.broadcasted_iota(jnp.int32, (rows, toks), 1)
    token = jnp.where(t_i // block == r_i, t_i % block, 4096)
    lane8 = lax.broadcasted_iota(jnp.int32, (8, 128), 1)
    scale = HEAD ** (-0.5)

    def attend(i, carry):
        bmax, bsum = carry
        for u in range(4):
            g = i * 4 + u
            at = pl.multiple_of(g * rows, rows)
            q = qblk[pl.ds(at, rows), :]
            k = kv_v[pl.ds(g * 4, 4), 0].reshape(toks, HEAD)
            v = kv_v[pl.ds(g * 4, 4), 1].reshape(toks, HEAD)
            s = lax.dot_general(q, k, (((1,), (1,)), ((), ())), preferred_element_type=F32) * scale
            n = count8[pl.ds(at, rows), :]
            ok = token < jnp.concatenate([n] * (toks // 128), axis=1)
            s = jnp.where(ok, s, NEG)
            m = jnp.max(s, axis=1, keepdims=True)
            e = jnp.where(ok, jnp.exp(s - m), 0.0)
            l = jnp.sum(e, axis=1, keepdims=True)
            outs[pl.ds(at, rows), :] = dot(e.astype(BF16), v)
            for c in range(4):
                here = lane8 == g * 4 + c
                bmax = jnp.where(here, m[c * 8 : (c + 1) * 8], bmax)
                bsum = jnp.where(here, l[c * 8 : (c + 1) * 8], bsum)
        return bmax, bsum

    zero8 = jnp.zeros((8, 128), F32)
    bmax, bsum = lax.fori_loop(0, blocks // 16, attend, (zero8, zero8))

    lane_r = lax.broadcasted_iota(jnp.int32, (num_req, 128), 1)
    tops = jnp.zeros((num_req, 128), F32)
    sums = jnp.zeros((num_req, 128), F32)
    for h in range(group):
        high = jnp.where(owns, bmax[h : h + 1, :], NEG)
        top = jnp.max(high, axis=1, keepdims=True).astype(BF16).astype(F32)
        w = jnp.where(owns, jnp.exp(high - top), 0.0)
        total = jnp.sum(w * bsum[h : h + 1, :], axis=1, keepdims=True)
        w_hi, w_lo = split(w)
        o_hi, o_lo = split(outs[pl.ds(h, blocks, stride=8), :])
        acc = dot(w_hi, o_hi) + dot(w_hi, o_lo) + dot(w_lo, o_hi)
        msgf[pl.ds(h, num_req, stride=8), :] = acc
        tops = jnp.where(lane_r == h, top, tops)
        sums = jnp.where(lane_r == h, total, sums)
    sum_hi = sums.astype(BF16).astype(F32)
    msgf[pl.ds(group, num_req, stride=8), :] = tops
    msgf[pl.ds(group + 1, num_req, stride=8), :] = sum_hi
    msgf[pl.ds(group + 2, num_req, stride=8), :] = sums - sum_hi
    msg[...] = msgf[...].reshape(num_req, 8, 128).astype(BF16)
    recv[me] = msg[me]

    def send_part(j, carry):
        peer = peer_of(j)
        pltpu.make_async_remote_copy(
            src_ref=msg.at[peer], dst_ref=recv.at[me], send_sem=ms_sem, recv_sem=mr_sem,
            device_id={"blk": peer}, device_id_type=MESH,
        ).start()
        return carry

    lax.fori_loop(0, num_blk - 1, send_part, 0)
    for load in loads[4:]:
        load.wait()
    pltpu.make_async_copy(recv.at[others], recv.at[others], mr_sem).wait()

    recvf[...] = recv[...].astype(F32).reshape(num_blk * 8, 128)
    tops = recvf[pl.ds(group, num_blk, stride=8), :]
    sums = recvf[pl.ds(group + 1, num_blk, stride=8), :] + recvf[pl.ds(group + 2, num_blk, stride=8), :]
    w = jnp.exp(tops - jnp.max(tops, axis=0, keepdims=True))
    total = jnp.sum(w * sums, axis=0, keepdims=True)
    heads = []
    for h in range(group):
        acc = jnp.sum(w[:, h : h + 1] * recvf[pl.ds(h, num_blk, stride=8), :], axis=0, keepdims=True)
        heads.append(acc / total[:, h : h + 1])
    attn = jnp.concatenate(heads, axis=1)
    attn8 = jnp.broadcast_to(attn, (8, group * HEAD)).astype(BF16)
    hbuf[kv] = dot(attn8, wo_v[...])[:1, :]
    own = pl.ds(pl.multiple_of(kv * cols, 128), cols)
    hbuf[kv, :, own] = hbuf[kv, :, own] + res_v[...].astype(F32)

    hops = []
    for j in range(1, num_kv):
        hops.append(pltpu.make_async_remote_copy(
            src_ref=hbuf.at[kv], dst_ref=hbuf.at[kv], send_sem=hs_sem.at[j - 1], recv_sem=hr_sem.at[j - 1],
            device_id={"kv": lax.rem(kv + j, num_kv)}, device_id_type=MESH,
        ))
    for hop in hops:
        hop.start()
    for hop in hops:
        hop.wait_recv()

    hidden = hbuf[0]
    for j in range(1, num_kv):
        hidden = hidden + hbuf[j]
    hsum[...] = hidden
    inverse = lax.rsqrt(jnp.sum(hidden * hidden, axis=1, keepdims=True) / width + 1e-05)
    normed = hidden * inverse * gain_v[...].astype(F32)
    normed8 = jnp.broadcast_to(normed, (8, width)).astype(BF16)
    next_ref[...] = dot(normed8, wq_v[...])[:1, :].astype(BF16)
    stream_ref[...] = hsum[:, own].astype(BF16)

    for hop in hops:
        hop.wait_send()
    pltpu.make_async_copy(qall.at[others], qall.at[others], qs_sem).wait()
    pltpu.make_async_copy(recv.at[others], recv.at[others], ms_sem).wait()


def per_device(num_blk, num_kv, queries, kv_pool, block_table, lengths, residual, out_weight, norm_gain, qkv_weight):
    group = queries.shape[1] // HEAD
    num_req, max_blocks = block_table.shape
    blocks, _, block, _ = kv_pool.shape
    width = out_weight.shape[1]
    cols = residual.shape[1]
    out_cols = qkv_weight.shape[1]
    anywhere = pl.BlockSpec(memory_space=pl.ANY)
    vmem = pl.BlockSpec(memory_space=pltpu.VMEM)
    dma = pltpu.SemaphoreType.DMA
    return pl.pallas_call(
        functools.partial(kernel, num_blk, num_kv, group),
        out_shape=(
            jax.ShapeDtypeStruct((1, cols), BF16),
            jax.ShapeDtypeStruct((1, out_cols), BF16),
        ),
        in_specs=[anywhere] * 8,
        out_specs=(vmem, vmem),
        scratch_shapes=[
            pltpu.VMEM(queries.shape, BF16),
            pltpu.VMEM(kv_pool.shape, BF16),
            pltpu.VMEM(block_table.shape, jnp.int32),
            pltpu.SMEM((num_req,), jnp.int32),
            pltpu.VMEM(residual.shape, BF16),
            pltpu.VMEM(out_weight.shape, BF16),
            pltpu.VMEM((1, width), BF16),
            pltpu.VMEM(qkv_weight.shape, BF16),
            pltpu.VMEM((8, HEAD), BF16),
            pltpu.VMEM((num_req, 8, HEAD), BF16),
            pltpu.VMEM((blocks, 128), F32),
            pltpu.VMEM((blocks * 8, num_req * 8), BF16),
            pltpu.VMEM((blocks * 8, 128), jnp.int32),
            pltpu.VMEM((blocks * 8, HEAD), BF16),
            pltpu.VMEM((blocks * 8, HEAD), F32),
            pltpu.VMEM((num_req * 8, HEAD), F32),
            pltpu.VMEM((num_req, 8, HEAD), BF16),
            pltpu.VMEM((num_blk, 8, HEAD), BF16),
            pltpu.VMEM((num_blk * 8, HEAD), F32),
            pltpu.VMEM((num_kv, 1, width), F32),
            pltpu.VMEM((1, width), F32),
            dma((8,)), dma, dma, dma, dma, dma((num_kv - 1,)), dma((num_kv - 1,)),
        ],
        compiler_params=pltpu.CompilerParams(
            collective_id=0, has_side_effects=True, vmem_limit_bytes=60 * 1024 * 1024
        ),
    )(queries, kv_pool, block_table, lengths, residual, out_weight, norm_gain.reshape(1, -1), qkv_weight)


def solution(mesh):
    placed = (
        P("blk", "kv"),
        P("blk", None, None, "kv"),
        P(),
        P(),
        P("blk", "kv"),
        P("kv", None),
        P(),
        P(None, "kv"),
    )
    return jax.shard_map(
        functools.partial(per_device, mesh.shape["blk"], mesh.shape["kv"]),
        mesh=mesh,
        in_specs=placed,
        out_specs=(P("blk", "kv"), P("blk", "kv")),
        check_vma=False,
    )
```

```python
import functools

import jax
import jax.numpy as jnp
from jax import lax
from jax.experimental import pallas as pl
from jax.experimental.pallas import tpu as pltpu
from jax.sharding import PartitionSpec as P

HEAD = 128
MESH = pl.DeviceIdType.MESH
F32 = jnp.float32
BF16 = jnp.bfloat16
NEG = -1e30
INNER = 8


def rows_of(x, count, width):
    rows = [x[:, i * width : (i + 1) * width] for i in range(count)]
    rows.append(jnp.zeros((8 - count, width), x.dtype))
    return jnp.concatenate(rows, axis=0)


def split(x):
    hi = x.astype(BF16)
    return hi, (x - hi.astype(F32)).astype(BF16)


def dot(a, b):
    return jnp.dot(a, b, preferred_element_type=F32)


def kernel(
    num_blk, inner, num_kv, group,
    q_hbm, kv_hbm, table_hbm, len_hbm, res_hbm, wo_hbm, gain_hbm, wq_hbm,
    stream_ref, next_ref,
    q_v, kv_v, table_v, len_s, res_v, wo_v, gain_v, wq_v,
    qall, code_v, expand, count8, qblk, outs, msgf, msg, recv, recvf, hbuf, hsum,
    local_sem, qs_sem, qr_sem, ms_sem, mr_sem, hs_sem, hr_sem,
):
    me = lax.axis_index("blk")
    num_ring = num_blk // inner
    ring = me // inner
    spot = lax.rem(me, inner)
    near = sorted(range(1, num_ring), key=lambda k: min(k, num_ring - k))
    kv = lax.axis_index("kv")
    num_req = qall.shape[0]
    blocks = kv_v.shape[0]
    block = kv_v.shape[2]
    width = hsum.shape[1]
    cols = res_v.shape[1]

    pairs = [
        (q_hbm, q_v), (table_hbm, table_v), (len_hbm, len_s), (kv_hbm, kv_v),
        (res_hbm, res_v), (gain_hbm, gain_v), (wo_hbm, wo_v), (wq_hbm, wq_v),
    ]
    loads = [pltpu.make_async_copy(a, b, local_sem.at[i]) for i, (a, b) in enumerate(pairs)]

    def peer_of(j):
        step = num_blk // 2 + (1 - 2 * (j % 2)) * ((j + 1) // 2)
        return lax.rem(me + step, num_blk)

    barrier = pltpu.get_barrier_semaphore()
    loads[0].start()
    loads[1].start()
    loads[2].start()

    def along(k):
        return {"blk": lax.rem(ring + k, num_ring) * inner + spot}

    def across(k):
        return {"blk": ring * inner + lax.rem(spot + k, inner)}

    for k in near:
        pl.semaphore_signal(barrier, inc=1, device_id=along(k), device_id_type=MESH)
    for k in range(1, inner):
        pl.semaphore_signal(barrier, inc=1, device_id=across(k), device_id_type=MESH)
    for k in range(1, num_kv):
        pl.semaphore_signal(
            barrier, inc=1, device_id={"kv": lax.rem(kv + k, num_kv)}, device_id_type=MESH
        )
    for load in loads[3:]:
        load.start()

    loads[0].wait()
    mine = rows_of(q_v[...].astype(F32), group, HEAD).astype(BF16)
    qall[me] = mine

    loads[1].wait()
    loads[2].wait()
    max_blocks = table_v.shape[1]
    lane = lax.broadcasted_iota(jnp.int32, (1, 128), 1)
    row_id = lax.broadcasted_iota(jnp.int32, (blocks, 128), 0)
    best = jnp.full((blocks, 128), -1.0, F32)
    first = me * blocks
    for part in range(max_blocks // 128):
        at = lane + part * 128

        def match(i, acc):
            local = table_v[pl.ds(pl.multiple_of(i * 8, 8), 8), part * 128 : (part + 1) * 128] - first
            for c in range(8):
                r = i * 8 + c
                tokens = jnp.clip(len_s[r] - at * block, 0, block)
                code = (tokens + r * 128).astype(F32)
                acc = jnp.where(row_id == local[c : c + 1, :], code, acc)
            return acc

        best = lax.fori_loop(0, num_req // 8, match, best)
    code = jnp.broadcast_to(jnp.max(best, axis=1, keepdims=True), (blocks, 128))
    code_v[...] = code
    code_row = jnp.transpose(code)[:num_req, :].astype(jnp.int32)
    owns = (code_row >> 7) == lax.broadcasted_iota(jnp.int32, (num_req, blocks), 0)

    column = lax.broadcasted_iota(jnp.int32, (16, num_req * 8), 1)
    sub = lax.broadcasted_iota(jnp.int32, (16, 128), 0)

    def widen(i, carry):
        a = jnp.broadcast_to(code_v[pl.ds(2 * i, 1), :], (16, 128))
        b = jnp.broadcast_to(code_v[pl.ds(2 * i + 1, 1), :], (16, 128))
        both = jnp.where(sub < 8, a, b).astype(jnp.int32)
        target = (both >> 7) * 8 + (sub & 7)
        wide = jnp.concatenate([target] * (num_req * 8 // 128), axis=1)
        at16 = pl.multiple_of(i * 16, 16)
        expand[pl.ds(at16, 16), :] = jnp.where(column == wide, 1.0, 0.0).astype(BF16)
        count8[pl.ds(at16, 16), :] = jnp.where(both >= 0, both & 127, 0)
        return carry

    lax.fori_loop(0, blocks // 2, widen, 0, unroll=4)

    pl.semaphore_wait(barrier, num_ring - 1 + inner - 1 + num_kv - 1)

    def query(slot, k, device, send, arrive):
        return pltpu.make_async_remote_copy(
            src_ref=qall.at[slot], dst_ref=qall.at[slot], send_sem=send, recv_sem=arrive,
            device_id=device, device_id_type=MESH,
        )

    ahead = [query(me, k, along(k), qs_sem.at[k], qr_sem.at[k]) for k in near]
    for copy in ahead[::-1]:
        copy.start()
    for k in range(1, inner):
        query(me, k, across(k), qs_sem.at[0], qr_sem.at[0]).start()
    for k, copy in zip(near, ahead):
        copy.wait_recv()
        source = lax.rem(ring + num_ring - k, num_ring) * inner + spot
        for c in range(1, inner):
            query(source, c, across(c), qs_sem.at[0], qr_sem.at[0]).start()
    loads[3].wait()
    others = pl.ds(0, num_blk - 1)
    passed = pl.ds(0, (inner - 1) * num_ring)
    pltpu.make_async_copy(qall.at[passed], qall.at[passed], qr_sem.at[0]).wait()

    flat = qall[...].astype(F32).reshape(num_req * 8, HEAD).astype(BF16)
    qblk[...] = dot(expand[...], flat).astype(BF16)

    rows = 32
    toks = 4 * block
    r_i = lax.broadcasted_iota(jnp.int32, (rows, toks), 0) // 8
    t_i = lax.broadcasted_iota(jnp.int32, (rows, toks), 1)
    token = jnp.where(t_i // block == r_i, t_i % block, 4096)
    lane8 = lax.broadcasted_iota(jnp.int32, (8, 128), 1)
    scale = HEAD ** (-0.5)
    groups = blocks // 4
    scores = []
    for g in range(groups):
        q = qblk[g * rows : (g + 1) * rows, :]
        k = kv_v[g * 4 : (g + 1) * 4, 0].reshape(toks, HEAD)
        scores.append(lax.dot_general(q, k, (((1,), (1,)), ((), ())), preferred_element_type=F32))
    bmax = jnp.zeros((8, 128), F32)
    bsum = jnp.zeros((8, 128), F32)
    weights = []
    for g in range(groups):
        n = count8[g * rows : (g + 1) * rows, :]
        ok = token < jnp.concatenate([n] * (toks // 128), axis=1)
        s = jnp.where(ok, scores[g] * scale, NEG)
        m = jnp.max(s, axis=1, keepdims=True)
        e = jnp.exp(s - m)
        l = jnp.sum(e, axis=1, keepdims=True)
        weights.append(e.astype(BF16))
        for c in range(4):
            here = lane8 == g * 4 + c
            bmax = jnp.where(here, m[c * 8 : (c + 1) * 8], bmax)
            bsum = jnp.where(here, l[c * 8 : (c + 1) * 8], bsum)
    for g in range(groups):
        v = kv_v[g * 4 : (g + 1) * 4, 1].reshape(toks, HEAD)
        outs[g * rows : (g + 1) * rows, :] = dot(weights[g], v)

    lane_r = lax.broadcasted_iota(jnp.int32, (num_req, 128), 1)
    tops = jnp.zeros((num_req, 128), F32)
    sums = jnp.zeros((num_req, 128), F32)
    for h in range(group):
        high = jnp.where(owns, bmax[h : h + 1, :], NEG)
        top = jnp.max(high, axis=1, keepdims=True).astype(BF16).astype(F32)
        w = jnp.where(owns, jnp.exp(high - top), 0.0)
        total = jnp.sum(w * bsum[h : h + 1, :], axis=1, keepdims=True)
        w_hi, w_lo = split(w)
        o_hi, o_lo = split(outs[pl.ds(h, blocks, stride=8), :])
        acc = dot(w_hi, o_hi) + dot(w_hi, o_lo) + dot(w_lo, o_hi)
        msgf[pl.ds(h, num_req, stride=8), :] = acc
        tops = jnp.where(lane_r == h, top, tops)
        sums = jnp.where(lane_r == h, total, sums)
    sum_hi = sums.astype(BF16).astype(F32)
    msgf[pl.ds(group, num_req, stride=8), :] = tops
    msgf[pl.ds(group + 1, num_req, stride=8), :] = sum_hi
    msgf[pl.ds(group + 2, num_req, stride=8), :] = sums - sum_hi
    msg[...] = msgf[...].reshape(num_req, 8, 128).astype(BF16)
    recv[me] = msg[me]

    def send_part(j, carry):
        peer = peer_of(j)
        pltpu.make_async_remote_copy(
            src_ref=msg.at[peer], dst_ref=recv.at[me], send_sem=ms_sem, recv_sem=mr_sem,
            device_id={"blk": peer}, device_id_type=MESH,
        ).start()
        return carry

    lax.fori_loop(0, num_blk - 1, send_part, 0)
    for load in loads[4:]:
        load.wait()
    pltpu.make_async_copy(recv.at[others], recv.at[others], mr_sem).wait()

    gain = gain_v[...].astype(F32)
    gain = jnp.concatenate([gain[i : i + 1, :] for i in range(width // 128)], axis=1)
    recvf[...] = recv[...].astype(F32).reshape(num_blk * 8, 128)
    tops = recvf[pl.ds(group, num_blk, stride=8), :]
    sums = recvf[pl.ds(group + 1, num_blk, stride=8), :] + recvf[pl.ds(group + 2, num_blk, stride=8), :]
    w = jnp.exp(tops - jnp.max(tops, axis=0, keepdims=True))
    total = jnp.sum(w * sums, axis=0, keepdims=True)
    heads = []
    for h in range(group):
        acc = jnp.sum(w[:, h : h + 1] * recvf[pl.ds(h, num_blk, stride=8), :], axis=0, keepdims=True)
        heads.append(acc / total[:, h : h + 1])
    attn = jnp.concatenate(heads, axis=1)
    attn8 = jnp.broadcast_to(attn, (8, group * HEAD)).astype(BF16)
    hbuf[kv] = dot(attn8, wo_v[...])[:1, :]
    own = pl.ds(pl.multiple_of(kv * cols, 128), cols)
    hbuf[kv, :, own] = hbuf[kv, :, own] + res_v[...].astype(F32)

    hops = []
    for j in range(1, num_kv):
        hops.append(pltpu.make_async_remote_copy(
            src_ref=hbuf.at[kv], dst_ref=hbuf.at[kv], send_sem=hs_sem.at[j - 1], recv_sem=hr_sem.at[j - 1],
            device_id={"kv": lax.rem(kv + j, num_kv)}, device_id_type=MESH,
        ))
    for hop in hops:
        hop.start()
    for hop in hops:
        hop.wait_recv()

    hidden = hbuf[0]
    for j in range(1, num_kv):
        hidden = hidden + hbuf[j]
    hsum[...] = hidden
    inverse = lax.rsqrt(jnp.sum(hidden * hidden, axis=1, keepdims=True) / width + 1e-05)
    normed = hidden * inverse * gain
    normed8 = jnp.broadcast_to(normed, (8, width)).astype(BF16)
    next_ref[...] = dot(normed8, wq_v[...])[:1, :].astype(BF16)
    stream_ref[...] = hsum[:, own].astype(BF16)

    for hop in hops:
        hop.wait_send()
    for copy in ahead:
        copy.wait_send()
    pltpu.make_async_copy(qall.at[passed], qall.at[passed], qs_sem.at[0]).wait()
    pltpu.make_async_copy(recv.at[others], recv.at[others], ms_sem).wait()


def per_device(num_blk, inner, num_kv, queries, kv_pool, block_table, lengths, residual, out_weight, norm_gain, qkv_weight):
    group = queries.shape[1] // HEAD
    num_req, max_blocks = block_table.shape
    blocks, _, block, _ = kv_pool.shape
    width = out_weight.shape[1]
    cols = residual.shape[1]
    out_cols = qkv_weight.shape[1]
    anywhere = pl.BlockSpec(memory_space=pl.ANY)
    vmem = pl.BlockSpec(memory_space=pltpu.VMEM)
    dma = pltpu.SemaphoreType.DMA
    return pl.pallas_call(
        functools.partial(kernel, num_blk, inner, num_kv, group),
        out_shape=(
            jax.ShapeDtypeStruct((1, cols), BF16),
            jax.ShapeDtypeStruct((1, out_cols), BF16),
        ),
        in_specs=[anywhere] * 8,
        out_specs=(vmem, vmem),
        scratch_shapes=[
            pltpu.VMEM(queries.shape, BF16),
            pltpu.VMEM(kv_pool.shape, BF16),
            pltpu.VMEM(block_table.shape, jnp.int32),
            pltpu.SMEM((num_req,), jnp.int32),
            pltpu.VMEM(residual.shape, BF16),
            pltpu.VMEM(out_weight.shape, BF16),
            pltpu.VMEM((width // 128, 128), BF16),
            pltpu.VMEM(qkv_weight.shape, BF16),
            pltpu.VMEM((num_req, 8, HEAD), BF16),
            pltpu.VMEM((blocks, 128), F32),
            pltpu.VMEM((blocks * 8, num_req * 8), BF16),
            pltpu.VMEM((blocks * 8, 128), jnp.int32),
            pltpu.VMEM((blocks * 8, HEAD), BF16),
            pltpu.VMEM((blocks * 8, HEAD), F32),
            pltpu.VMEM((num_req * 8, HEAD), F32),
            pltpu.VMEM((num_req, 8, HEAD), BF16),
            pltpu.VMEM((num_blk, 8, HEAD), BF16),
            pltpu.VMEM((num_blk * 8, HEAD), F32),
            pltpu.VMEM((num_kv, 1, width), F32),
            pltpu.VMEM((1, width), F32),
            dma((8,)), dma((num_blk // inner,)), dma((num_blk // inner,)), dma, dma, dma((num_kv - 1,)), dma((num_kv - 1,)),
        ],
        compiler_params=pltpu.CompilerParams(
            collective_id=0, has_side_effects=True, vmem_limit_bytes=60 * 1024 * 1024
        ),
    )(queries, kv_pool, block_table, lengths, residual, out_weight, norm_gain.reshape(-1, 128), qkv_weight)


def solution(mesh):
    placed = (
        P("blk", "kv"),
        P("blk", None, None, "kv"),
        P(),
        P(),
        P("blk", "kv"),
        P("kv", None),
        P(),
        P(None, "kv"),
    )
    return jax.shard_map(
        functools.partial(per_device, mesh.shape["blk"], INNER, mesh.shape["kv"]),
        mesh=mesh,
        in_specs=placed,
        out_specs=(P("blk", "kv"), P("blk", "kv")),
        check_vma=False,
    )
```

```python
import functools

import jax
import jax.numpy as jnp
from jax import lax
from jax.experimental import pallas as pl
from jax.experimental.pallas import tpu as pltpu
from jax.sharding import PartitionSpec as P

HEAD = 128
MESH = pl.DeviceIdType.MESH
F32 = jnp.float32
BF16 = jnp.bfloat16
NEG = -1e30
CHIPS_X = 4


def rows_of(x, count, width):
    rows = [x[:, i * width : (i + 1) * width] for i in range(count)]
    rows.append(jnp.zeros((8 - count, width), x.dtype))
    return jnp.concatenate(rows, axis=0)


def split(x):
    hi = x.astype(BF16)
    return hi, (x - hi.astype(F32)).astype(BF16)


def dot(a, b):
    return jnp.dot(a, b, preferred_element_type=F32)


def kernel(
    num_blk, num_x, num_kv, group,
    q_hbm, kv_hbm, table_hbm, len_hbm, res_hbm, wo_hbm, gain_hbm, wq_hbm,
    both_ref,
    q_v, kv_v, table_v, len_s, res_v, wo_v, gain_v, wq_v,
    qall, code_v, expand, count8, qblk, outs, msgf, msg, recv, recvf, hbuf, hsum,
    local_sem, ready, qs_sem, qr_sem, ms_sem, mr_sem, hs_sem, hr_sem,
):
    me = lax.axis_index("blk")
    kv = lax.axis_index("kv")
    num_z = num_blk // (num_x * 2)
    core = lax.rem(me, 2)
    x_at = [lax.rem(me // 2 + k, num_x) * 2 for k in range(num_x)]
    z_at = [lax.rem(me // (num_x * 2) + k, num_z) * (num_x * 2) for k in range(num_z)]
    core_at = [core, 1 - core]

    def peer(k):
        return z_at[k[0]] + x_at[k[1]] + core_at[k[2]]

    def hops(k):
        return min(k[0], num_z - k[0]) + min(k[1], num_x - k[1]) + 0.1 * k[2]

    others = [(a, b, c) for a in range(num_z) for b in range(num_x) for c in range(2)][1:]
    others.sort(key=hops, reverse=True)
    plane = [k for k in others if k[0] == 0]
    column = [k for k in others if k[1:] == (0, 0)]
    rest = [k for k in others if k not in plane and k not in column]
    num_req = qall.shape[0]
    blocks = kv_v.shape[0]
    block = kv_v.shape[2]
    width = hsum.shape[1]
    cols = res_v.shape[1]

    pairs = [
        (q_hbm, q_v), (table_hbm, table_v), (len_hbm, len_s), (kv_hbm, kv_v),
        (res_hbm, res_v), (gain_hbm, gain_v), (wo_hbm, wo_v), (wq_hbm, wq_v),
    ]
    loads = [pltpu.make_async_copy(a, b, local_sem.at[i]) for i, (a, b) in enumerate(pairs)]

    barrier = pltpu.get_barrier_semaphore()
    loads[0].start()
    loads[1].start()
    loads[2].start()

    for k in column + plane:
        pl.semaphore_signal(barrier, inc=1, device_id={"blk": peer(k)}, device_id_type=MESH)
    for k in range(1, num_kv):
        pl.semaphore_signal(
            barrier, inc=1, device_id={"kv": lax.rem(kv + k, num_kv)}, device_id_type=MESH
        )
    for load in loads[3:]:
        load.start()

    loads[0].wait()
    mine = rows_of(q_v[...].astype(F32), group, HEAD).astype(BF16)
    qall[me] = mine

    loads[1].wait()
    loads[2].wait()
    max_blocks = table_v.shape[1]
    lane = lax.broadcasted_iota(jnp.int32, (1, 128), 1)
    row_id = lax.broadcasted_iota(jnp.int32, (blocks, 128), 0)
    best = jnp.full((blocks, 128), -1.0, F32)
    first = me * blocks
    for part in range(max_blocks // 128):
        at = lane + part * 128

        def match(i, acc):
            local = table_v[pl.ds(pl.multiple_of(i * 8, 8), 8), part * 128 : (part + 1) * 128] - first
            for c in range(8):
                r = i * 8 + c
                tokens = jnp.clip(len_s[r] - at * block, 0, block)
                code = (tokens + r * 128).astype(F32)
                acc = jnp.where(row_id == local[c : c + 1, :], code, acc)
            return acc

        best = lax.fori_loop(0, num_req // 8, match, best)
    code = jnp.broadcast_to(jnp.max(best, axis=1, keepdims=True), (blocks, 128))
    code_v[...] = code
    code_row = jnp.transpose(code)[:num_req, :].astype(jnp.int32)
    owns = (code_row >> 7) == lax.broadcasted_iota(jnp.int32, (num_req, blocks), 0)

    col_id = lax.broadcasted_iota(jnp.int32, (16, num_req * 8), 1)
    sub = lax.broadcasted_iota(jnp.int32, (16, 128), 0)

    def widen(i, carry):
        a = jnp.broadcast_to(code_v[pl.ds(2 * i, 1), :], (16, 128))
        b = jnp.broadcast_to(code_v[pl.ds(2 * i + 1, 1), :], (16, 128))
        both = jnp.where(sub < 8, a, b).astype(jnp.int32)
        target = (both >> 7) * 8 + (sub & 7)
        wide = jnp.concatenate([target] * (num_req * 8 // 128), axis=1)
        at16 = pl.multiple_of(i * 16, 16)
        expand[pl.ds(at16, 16), :] = jnp.where(col_id == wide, 1.0, 0.0).astype(BF16)
        count8[pl.ds(at16, 16), :] = jnp.where(both >= 0, both & 127, 0)
        return carry

    lax.fori_loop(0, blocks // 2, widen, 0, unroll=4)

    pl.semaphore_wait(barrier, len(column) + len(plane) + num_kv - 1)

    for k in plane:
        pl.semaphore_signal(ready, inc=1, device_id={"blk": peer(k)}, device_id_type=MESH)

    def send_query(k):
        pltpu.make_async_remote_copy(
            src_ref=qall.at[me], dst_ref=qall.at[me], send_sem=qs_sem, recv_sem=qr_sem,
            device_id={"blk": peer(k)}, device_id_type=MESH,
        ).start()

    for k in column + plane:
        send_query(k)
    pl.semaphore_wait(ready, len(plane))
    for k in rest:
        send_query(k)
    loads[3].wait()
    rows63 = pl.ds(0, num_blk - 1)
    pltpu.make_async_copy(qall.at[rows63], qall.at[rows63], qr_sem).wait()

    flat = qall[...].astype(F32).reshape(num_req * 8, HEAD).astype(BF16)
    qblk[...] = dot(expand[...], flat).astype(BF16)

    rows = 32
    toks = 4 * block
    r_i = lax.broadcasted_iota(jnp.int32, (rows, toks), 0) // 8
    t_i = lax.broadcasted_iota(jnp.int32, (rows, toks), 1)
    token = jnp.where(t_i // block == r_i, t_i % block, 4096)
    lane8 = lax.broadcasted_iota(jnp.int32, (8, 128), 1)
    scale = HEAD ** (-0.5)
    groups = blocks // 4
    scores = []
    for g in range(groups):
        q = qblk[g * rows : (g + 1) * rows, :]
        k = kv_v[g * 4 : (g + 1) * 4, 0].reshape(toks, HEAD)
        scores.append(lax.dot_general(q, k, (((1,), (1,)), ((), ())), preferred_element_type=F32))
    bmax = jnp.zeros((8, 128), F32)
    bsum = jnp.zeros((8, 128), F32)
    weights = []
    for g in range(groups):
        n = count8[g * rows : (g + 1) * rows, :]
        ok = token < jnp.concatenate([n] * (toks // 128), axis=1)
        s = jnp.where(ok, scores[g] * scale, NEG)
        m = jnp.max(s, axis=1, keepdims=True)
        e = jnp.exp(s - m)
        l = jnp.sum(e, axis=1, keepdims=True)
        weights.append(e.astype(BF16))
        for c in range(4):
            here = lane8 == g * 4 + c
            bmax = jnp.where(here, m[c * 8 : (c + 1) * 8], bmax)
            bsum = jnp.where(here, l[c * 8 : (c + 1) * 8], bsum)
    for g in range(groups):
        v = kv_v[g * 4 : (g + 1) * 4, 1].reshape(toks, HEAD)
        outs[g * rows : (g + 1) * rows, :] = dot(weights[g], v)

    lane_r = lax.broadcasted_iota(jnp.int32, (num_req, 128), 1)
    tops = jnp.zeros((num_req, 128), F32)
    sums = jnp.zeros((num_req, 128), F32)
    for h in range(group):
        high = jnp.where(owns, bmax[h : h + 1, :], NEG)
        top = jnp.max(high, axis=1, keepdims=True).astype(BF16).astype(F32)
        w = jnp.where(owns, jnp.exp(high - top), 0.0)
        total = jnp.sum(w * bsum[h : h + 1, :], axis=1, keepdims=True)
        w_hi, w_lo = split(w)
        o_hi, o_lo = split(outs[pl.ds(h, blocks, stride=8), :])
        acc = dot(w_hi, o_hi) + dot(w_hi, o_lo) + dot(w_lo, o_hi)
        msgf[pl.ds(h, num_req, stride=8), :] = acc
        tops = jnp.where(lane_r == h, top, tops)
        sums = jnp.where(lane_r == h, total, sums)
    sum_hi = sums.astype(BF16).astype(F32)
    msgf[pl.ds(group, num_req, stride=8), :] = tops
    msgf[pl.ds(group + 1, num_req, stride=8), :] = sum_hi
    msgf[pl.ds(group + 2, num_req, stride=8), :] = sums - sum_hi
    msg[...] = msgf[...].reshape(num_req, 8, 128).astype(BF16)
    recv[me] = msg[me]

    for k in others:
        to = peer(k)
        pltpu.make_async_remote_copy(
            src_ref=msg.at[to], dst_ref=recv.at[me], send_sem=ms_sem, recv_sem=mr_sem,
            device_id={"blk": to}, device_id_type=MESH,
        ).start()
    for load in loads[4:]:
        load.wait()
    pltpu.make_async_copy(recv.at[rows63], recv.at[rows63], mr_sem).wait()

    gain = gain_v[...].astype(F32)
    gain = jnp.concatenate([gain[i : i + 1, :] for i in range(width // 128)], axis=1)
    recvf[...] = recv[...].astype(F32).reshape(num_blk * 8, 128)
    tops = recvf[pl.ds(group, num_blk, stride=8), :]
    sums = recvf[pl.ds(group + 1, num_blk, stride=8), :] + recvf[pl.ds(group + 2, num_blk, stride=8), :]
    w = jnp.exp(tops - jnp.max(tops, axis=0, keepdims=True))
    total = jnp.sum(w * sums, axis=0, keepdims=True)
    heads = []
    for h in range(group):
        acc = jnp.sum(w[:, h : h + 1] * recvf[pl.ds(h, num_blk, stride=8), :], axis=0, keepdims=True)
        heads.append(acc / total[:, h : h + 1])
    attn = jnp.concatenate(heads, axis=1)
    attn8 = jnp.broadcast_to(attn, (8, group * HEAD)).astype(BF16)
    hbuf[kv] = dot(attn8, wo_v[...])[:1, :]
    own = pl.ds(pl.multiple_of(kv * cols, 128), cols)
    hbuf[kv, :, own] = hbuf[kv, :, own] + res_v[...].astype(F32)

    hops_y = []
    for j in range(1, num_kv):
        hops_y.append(pltpu.make_async_remote_copy(
            src_ref=hbuf.at[kv], dst_ref=hbuf.at[kv], send_sem=hs_sem.at[j - 1], recv_sem=hr_sem.at[j - 1],
            device_id={"kv": lax.rem(kv + j, num_kv)}, device_id_type=MESH,
        ))
    for hop in hops_y:
        hop.start()
    for hop in hops_y:
        hop.wait_recv()

    hidden = hbuf[0]
    for j in range(1, num_kv):
        hidden = hidden + hbuf[j]
    hsum[...] = hidden
    inverse = lax.rsqrt(jnp.sum(hidden * hidden, axis=1, keepdims=True) / width + 1e-05)
    normed = hidden * inverse * gain
    normed8 = jnp.broadcast_to(normed, (8, width)).astype(BF16)
    both_ref[:, :cols] = hsum[:, own].astype(BF16)
    both_ref[:, cols:] = dot(normed8, wq_v[...])[:1, :].astype(BF16)

    for hop in hops_y:
        hop.wait_send()
    pltpu.make_async_copy(qall.at[rows63], qall.at[rows63], qs_sem).wait()
    pltpu.make_async_copy(recv.at[rows63], recv.at[rows63], ms_sem).wait()


def part(both_ref, stream_ref, next_ref):
    cols = stream_ref.shape[1]
    stream_ref[...] = both_ref[:, :cols]
    next_ref[...] = both_ref[:, cols:]


def per_device(num_blk, num_x, num_kv, queries, kv_pool, block_table, lengths, residual, out_weight, norm_gain, qkv_weight):
    group = queries.shape[1] // HEAD
    num_req, max_blocks = block_table.shape
    blocks, _, block, _ = kv_pool.shape
    width = out_weight.shape[1]
    cols = residual.shape[1]
    out_cols = qkv_weight.shape[1]
    anywhere = pl.BlockSpec(memory_space=pl.ANY)
    vmem = pl.BlockSpec(memory_space=pltpu.VMEM)
    dma = pltpu.SemaphoreType.DMA
    both = pl.pallas_call(
        functools.partial(kernel, num_blk, num_x, num_kv, group),
        out_shape=jax.ShapeDtypeStruct((1, cols + out_cols), BF16),
        in_specs=[anywhere] * 8,
        out_specs=vmem,
        scratch_shapes=[
            pltpu.VMEM(queries.shape, BF16),
            pltpu.VMEM(kv_pool.shape, BF16),
            pltpu.VMEM(block_table.shape, jnp.int32),
            pltpu.SMEM((num_req,), jnp.int32),
            pltpu.VMEM(residual.shape, BF16),
            pltpu.VMEM(out_weight.shape, BF16),
            pltpu.VMEM((width // 128, 128), BF16),
            pltpu.VMEM(qkv_weight.shape, BF16),
            pltpu.VMEM((num_req, 8, HEAD), BF16),
            pltpu.VMEM((blocks, 128), F32),
            pltpu.VMEM((blocks * 8, num_req * 8), BF16),
            pltpu.VMEM((blocks * 8, 128), jnp.int32),
            pltpu.VMEM((blocks * 8, HEAD), BF16),
            pltpu.VMEM((blocks * 8, HEAD), F32),
            pltpu.VMEM((num_req * 8, HEAD), F32),
            pltpu.VMEM((num_req, 8, HEAD), BF16),
            pltpu.VMEM((num_blk, 8, HEAD), BF16),
            pltpu.VMEM((num_blk * 8, HEAD), F32),
            pltpu.VMEM((num_kv, 1, width), F32),
            pltpu.VMEM((1, width), F32),
            dma((8,)), pltpu.SemaphoreType.REGULAR, dma, dma, dma, dma, dma((num_kv - 1,)), dma((num_kv - 1,)),
        ],
        compiler_params=pltpu.CompilerParams(
            collective_id=0, has_side_effects=True, vmem_limit_bytes=60 * 1024 * 1024
        ),
    )(queries, kv_pool, block_table, lengths, residual, out_weight, norm_gain.reshape(-1, 128), qkv_weight)
    return pl.pallas_call(
        part,
        out_shape=(
            jax.ShapeDtypeStruct((1, cols), BF16),
            jax.ShapeDtypeStruct((1, out_cols), BF16),
        ),
        in_specs=[vmem],
        out_specs=(vmem, vmem),
    )(both)


def solution(mesh):
    placed = (
        P("blk", "kv"),
        P("blk", None, None, "kv"),
        P(),
        P(),
        P("blk", "kv"),
        P("kv", None),
        P(),
        P(None, "kv"),
    )
    return jax.shard_map(
        functools.partial(per_device, mesh.shape["blk"], CHIPS_X, mesh.shape["kv"]),
        mesh=mesh,
        in_specs=placed,
        out_specs=(P("blk", "kv"), P("blk", "kv")),
        check_vma=False,
    )
```

```python
import functools

import jax
import jax.numpy as jnp
from jax import lax
from jax.experimental import pallas as pl
from jax.experimental.pallas import tpu as pltpu
from jax.sharding import PartitionSpec as P

HEAD = 128
MESH = pl.DeviceIdType.MESH
F32 = jnp.float32
BF16 = jnp.bfloat16
NEG = -1e30
CHIPS_X = 4


def rows_of(x, count, width):
    rows = [x[:, i * width : (i + 1) * width] for i in range(count)]
    rows.append(jnp.zeros((8 - count, width), x.dtype))
    return jnp.concatenate(rows, axis=0)


def split(x):
    hi = x.astype(BF16)
    return hi, (x - hi.astype(F32)).astype(BF16)


def dot(a, b):
    return jnp.dot(a, b, preferred_element_type=F32)


def kernel(
    num_blk, num_x, num_kv, group,
    q_hbm, kv_hbm, table_hbm, len_hbm, res_hbm, wo_hbm, gain_hbm, wq_hbm,
    both_ref,
    q_v, kv_v, table_v, len_s, res_v, wo_v, gain_v, wq_v,
    qall, code_v, expand, count8, qblk, outs, msgf, msg, recv, recvf, hbuf, hsum,
    local_sem, qs_sem, qr_sem, ms_sem, mr_sem, hs_sem, hr_sem,
):
    me = lax.axis_index("blk")
    kv = lax.axis_index("kv")
    num_z = num_blk // (num_x * 2)
    core = lax.rem(me, 2)
    x_at = [lax.rem(me // 2 + k, num_x) * 2 for k in range(num_x)]
    z_at = [lax.rem(me // (num_x * 2) + k, num_z) * (num_x * 2) for k in range(num_z)]
    core_at = [core, 1 - core]

    def peer(k):
        return z_at[k[0]] + x_at[k[1]] + core_at[k[2]]

    def hops(k):
        return min(k[0], num_z - k[0]) + min(k[1], num_x - k[1]) + 0.1 * k[2]

    others = [(a, b, c) for a in range(num_z) for b in range(num_x) for c in range(2)][1:]
    others.sort(key=hops, reverse=True)
    num_req = qall.shape[0]
    blocks = kv_v.shape[0]
    block = kv_v.shape[2]
    width = hsum.shape[1]
    cols = res_v.shape[1]

    pairs = [
        (q_hbm, q_v), (table_hbm, table_v), (len_hbm, len_s), (kv_hbm, kv_v),
        (res_hbm, res_v), (gain_hbm, gain_v), (wo_hbm, wo_v), (wq_hbm, wq_v),
    ]
    loads = [pltpu.make_async_copy(a, b, local_sem.at[i]) for i, (a, b) in enumerate(pairs)]

    sent = pl.ds(0, 6)
    qall[...] = jnp.zeros_like(qall)
    barrier = pltpu.get_barrier_semaphore()
    loads[0].start()
    loads[1].start()
    loads[2].start()

    for k in others:
        pl.semaphore_signal(barrier, inc=1, device_id={"blk": peer(k)}, device_id_type=MESH)
    for k in range(1, num_kv):
        pl.semaphore_signal(
            barrier, inc=1, device_id={"kv": lax.rem(kv + k, num_kv)}, device_id_type=MESH
        )
    for load in loads[3:]:
        load.start()

    loads[0].wait()
    mine = rows_of(q_v[...].astype(F32), group, HEAD).astype(BF16)
    qall[me] = mine

    loads[1].wait()
    loads[2].wait()
    max_blocks = table_v.shape[1]
    lane = lax.broadcasted_iota(jnp.int32, (1, 128), 1)
    row_id = lax.broadcasted_iota(jnp.int32, (blocks, 128), 0)
    best = jnp.full((blocks, 128), -1.0, F32)
    first = me * blocks
    for part in range(max_blocks // 128):
        at = lane + part * 128

        def match(i, acc):
            local = table_v[pl.ds(pl.multiple_of(i * 8, 8), 8), part * 128 : (part + 1) * 128] - first
            for c in range(8):
                r = i * 8 + c
                tokens = jnp.clip(len_s[r] - at * block, 0, block)
                code = (tokens + r * 128).astype(F32)
                acc = jnp.where(row_id == local[c : c + 1, :], code, acc)
            return acc

        best = lax.fori_loop(0, num_req // 8, match, best)
    code = jnp.broadcast_to(jnp.max(best, axis=1, keepdims=True), (blocks, 128))
    code_v[...] = code
    code_row = jnp.transpose(code)[:num_req, :].astype(jnp.int32)
    owns = (code_row >> 7) == lax.broadcasted_iota(jnp.int32, (num_req, blocks), 0)

    col_id = lax.broadcasted_iota(jnp.int32, (16, num_req * 8), 1)
    sub = lax.broadcasted_iota(jnp.int32, (16, 128), 0)

    def widen(i, carry):
        a = jnp.broadcast_to(code_v[pl.ds(2 * i, 1), :], (16, 128))
        b = jnp.broadcast_to(code_v[pl.ds(2 * i + 1, 1), :], (16, 128))
        both = jnp.where(sub < 8, a, b).astype(jnp.int32)
        target = (both >> 7) * 8 + (sub & 7)
        wide = jnp.concatenate([target] * (num_req * 8 // 128), axis=1)
        at16 = pl.multiple_of(i * 16, 16)
        expand[pl.ds(at16, 16), :] = jnp.where(col_id == wide, 1.0, 0.0).astype(BF16)
        count8[pl.ds(at16, 16), :] = jnp.where(both >= 0, both & 127, 0)
        return carry

    lax.fori_loop(0, blocks // 2, widen, 0, unroll=4)

    pl.semaphore_wait(barrier, num_blk - 1 + num_kv - 1)

    def send_query(k):
        pltpu.make_async_remote_copy(
            src_ref=qall.at[me, sent], dst_ref=qall.at[me, sent], send_sem=qs_sem, recv_sem=qr_sem,
            device_id={"blk": peer(k)}, device_id_type=MESH,
        ).start()

    for k in others:
        send_query(k)
    loads[3].wait()
    rows63 = pl.ds(0, num_blk - 1)
    pltpu.make_async_copy(qall.at[rows63, sent], qall.at[rows63, sent], qr_sem).wait()

    flat = qall[...].astype(F32).reshape(num_req * 8, HEAD).astype(BF16)
    qblk[...] = dot(expand[...], flat).astype(BF16)

    rows = 32
    toks = 4 * block
    r_i = lax.broadcasted_iota(jnp.int32, (rows, toks), 0) // 8
    t_i = lax.broadcasted_iota(jnp.int32, (rows, toks), 1)
    token = jnp.where(t_i // block == r_i, t_i % block, 4096)
    lane8 = lax.broadcasted_iota(jnp.int32, (8, 128), 1)
    scale = HEAD ** (-0.5)
    groups = blocks // 4
    scores = []
    for g in range(groups):
        q = qblk[g * rows : (g + 1) * rows, :]
        k = kv_v[g * 4 : (g + 1) * 4, 0].reshape(toks, HEAD)
        scores.append(lax.dot_general(q, k, (((1,), (1,)), ((), ())), preferred_element_type=F32))
    bmax = jnp.zeros((8, 128), F32)
    bsum = jnp.zeros((8, 128), F32)
    weights = []
    for g in range(groups):
        n = count8[g * rows : (g + 1) * rows, :]
        ok = token < jnp.concatenate([n] * (toks // 128), axis=1)
        s = jnp.where(ok, scores[g] * scale, NEG)
        m = jnp.max(s, axis=1, keepdims=True)
        e = jnp.exp(s - m)
        l = jnp.sum(e, axis=1, keepdims=True)
        weights.append(e.astype(BF16))
        for c in range(4):
            here = lane8 == g * 4 + c
            bmax = jnp.where(here, m[c * 8 : (c + 1) * 8], bmax)
            bsum = jnp.where(here, l[c * 8 : (c + 1) * 8], bsum)
    for g in range(groups):
        v = kv_v[g * 4 : (g + 1) * 4, 1].reshape(toks, HEAD)
        outs[g * rows : (g + 1) * rows, :] = dot(weights[g], v)

    lane_r = lax.broadcasted_iota(jnp.int32, (num_req, 128), 1)
    stats = jnp.zeros((num_req, 128), F32)
    for h in range(group):
        high = jnp.where(owns, bmax[h : h + 1, :], NEG)
        top = jnp.max(high, axis=1, keepdims=True).astype(BF16).astype(F32)
        w = jnp.where(owns, jnp.exp(high - top), 0.0)
        total = jnp.sum(w * bsum[h : h + 1, :], axis=1, keepdims=True)
        w_hi, w_lo = split(w)
        o_hi, o_lo = split(outs[pl.ds(h, blocks, stride=8), :])
        acc = dot(w_hi, o_hi) + dot(w_hi, o_lo) + dot(w_lo, o_hi)
        msgf[pl.ds(h, num_req, stride=8), :] = acc
        sum_hi = total.astype(BF16).astype(F32)
        stats = jnp.where(lane_r == h, top, stats)
        stats = jnp.where(lane_r == h + 8, sum_hi, stats)
        stats = jnp.where(lane_r == h + 16, total - sum_hi, stats)
    msgf[pl.ds(group, num_req, stride=8), :] = stats
    msg[...] = msgf[...].reshape(num_req, 8, 128).astype(BF16)
    recv[me] = msg[me]

    for k in others:
        to = peer(k)
        pltpu.make_async_remote_copy(
            src_ref=msg.at[to, sent], dst_ref=recv.at[me, sent], send_sem=ms_sem, recv_sem=mr_sem,
            device_id={"blk": to}, device_id_type=MESH,
        ).start()
    for load in loads[4:]:
        load.wait()
    pltpu.make_async_copy(recv.at[rows63, sent], recv.at[rows63, sent], mr_sem).wait()

    gain = gain_v[...].astype(F32)
    gain = jnp.concatenate([gain[i : i + 1, :] for i in range(width // 128)], axis=1)
    recvf[...] = recv[...].astype(F32).reshape(num_blk * 8, 128)
    stats = recvf[pl.ds(group, num_blk, stride=8), :]
    sums = pltpu.roll(stats, 128 - 8, 1) + pltpu.roll(stats, 128 - 16, 1)
    tops = jnp.where(lane_r < group, stats, 0.0)
    w = jnp.exp(tops - jnp.max(tops, axis=0, keepdims=True))
    total = jnp.sum(w * sums, axis=0, keepdims=True)
    heads = []
    for h in range(group):
        acc = jnp.sum(w[:, h : h + 1] * recvf[pl.ds(h, num_blk, stride=8), :], axis=0, keepdims=True)
        heads.append(acc / total[:, h : h + 1])
    attn = jnp.concatenate(heads, axis=1)
    attn8 = jnp.broadcast_to(attn, (8, group * HEAD)).astype(BF16)
    hbuf[kv] = dot(attn8, wo_v[...])[:1, :]
    own = pl.ds(pl.multiple_of(kv * cols, 128), cols)
    hbuf[kv, :, own] = hbuf[kv, :, own] + res_v[...].astype(F32)

    hops_y = []
    for j in range(1, num_kv):
        hops_y.append(pltpu.make_async_remote_copy(
            src_ref=hbuf.at[kv], dst_ref=hbuf.at[kv], send_sem=hs_sem.at[j - 1], recv_sem=hr_sem.at[j - 1],
            device_id={"kv": lax.rem(kv + j, num_kv)}, device_id_type=MESH,
        ))
    for hop in hops_y:
        hop.start()
    for hop in hops_y:
        hop.wait_recv()

    hidden = hbuf[0]
    for j in range(1, num_kv):
        hidden = hidden + hbuf[j]
    hsum[...] = hidden
    inverse = lax.rsqrt(jnp.sum(hidden * hidden, axis=1, keepdims=True) / width + 1e-05)
    normed = hidden * inverse * gain
    normed8 = jnp.broadcast_to(normed, (8, width)).astype(BF16)
    both_ref[:, :cols] = hsum[:, own].astype(BF16)
    both_ref[:, cols:] = dot(normed8, wq_v[...])[:1, :].astype(BF16)

    for hop in hops_y:
        hop.wait_send()
    pltpu.make_async_copy(qall.at[rows63, sent], qall.at[rows63, sent], qs_sem).wait()
    pltpu.make_async_copy(recv.at[rows63, sent], recv.at[rows63, sent], ms_sem).wait()


def part(both_ref, stream_ref, next_ref):
    cols = stream_ref.shape[1]
    stream_ref[...] = both_ref[:, :cols]
    next_ref[...] = both_ref[:, cols:]


def per_device(num_blk, num_x, num_kv, queries, kv_pool, block_table, lengths, residual, out_weight, norm_gain, qkv_weight):
    group = queries.shape[1] // HEAD
    num_req, max_blocks = block_table.shape
    blocks, _, block, _ = kv_pool.shape
    width = out_weight.shape[1]
    cols = residual.shape[1]
    out_cols = qkv_weight.shape[1]
    anywhere = pl.BlockSpec(memory_space=pl.ANY)
    vmem = pl.BlockSpec(memory_space=pltpu.VMEM)
    dma = pltpu.SemaphoreType.DMA
    both = pl.pallas_call(
        functools.partial(kernel, num_blk, num_x, num_kv, group),
        out_shape=jax.ShapeDtypeStruct((1, cols + out_cols), BF16),
        in_specs=[anywhere] * 8,
        out_specs=vmem,
        scratch_shapes=[
            pltpu.VMEM(queries.shape, BF16),
            pltpu.VMEM(kv_pool.shape, BF16),
            pltpu.VMEM(block_table.shape, jnp.int32),
            pltpu.SMEM((num_req,), jnp.int32),
            pltpu.VMEM(residual.shape, BF16),
            pltpu.VMEM(out_weight.shape, BF16),
            pltpu.VMEM((width // 128, 128), BF16),
            pltpu.VMEM(qkv_weight.shape, BF16),
            pltpu.VMEM((num_req, 8, HEAD), BF16),
            pltpu.VMEM((blocks, 128), F32),
            pltpu.VMEM((blocks * 8, num_req * 8), BF16),
            pltpu.VMEM((blocks * 8, 128), jnp.int32),
            pltpu.VMEM((blocks * 8, HEAD), BF16),
            pltpu.VMEM((blocks * 8, HEAD), F32),
            pltpu.VMEM((num_req * 8, HEAD), F32),
            pltpu.VMEM((num_req, 8, HEAD), BF16),
            pltpu.VMEM((num_blk, 8, HEAD), BF16),
            pltpu.VMEM((num_blk * 8, HEAD), F32),
            pltpu.VMEM((num_kv, 1, width), F32),
            pltpu.VMEM((1, width), F32),
            dma((8,)), dma, dma, dma, dma, dma((num_kv - 1,)), dma((num_kv - 1,)),
        ],
        compiler_params=pltpu.CompilerParams(
            collective_id=0, has_side_effects=True, vmem_limit_bytes=60 * 1024 * 1024
        ),
    )(queries, kv_pool, block_table, lengths, residual, out_weight, norm_gain.reshape(-1, 128), qkv_weight)
    return pl.pallas_call(
        part,
        out_shape=(
            jax.ShapeDtypeStruct((1, cols), BF16),
            jax.ShapeDtypeStruct((1, out_cols), BF16),
        ),
        in_specs=[vmem],
        out_specs=(vmem, vmem),
    )(both)


def solution(mesh):
    placed = (
        P("blk", "kv"),
        P("blk", None, None, "kv"),
        P(),
        P(),
        P("blk", "kv"),
        P("kv", None),
        P(),
        P(None, "kv"),
    )
    return jax.shard_map(
        functools.partial(per_device, mesh.shape["blk"], CHIPS_X, mesh.shape["kv"]),
        mesh=mesh,
        in_specs=placed,
        out_specs=(P("blk", "kv"), P("blk", "kv")),
        check_vma=False,
    )
```

```python
import functools

import jax
import jax.numpy as jnp
from jax import lax
from jax.experimental import pallas as pl
from jax.experimental.pallas import tpu as pltpu
from jax.sharding import PartitionSpec as P

HEAD = 128
MESH = pl.DeviceIdType.MESH
F32 = jnp.float32
BF16 = jnp.bfloat16
NEG = -1e30
CHIPS_X = 4


def rows_of(x, count, width):
    rows = [x[:, i * width : (i + 1) * width] for i in range(count)]
    rows.append(jnp.zeros((8 - count, width), x.dtype))
    return jnp.concatenate(rows, axis=0)


def split(x):
    hi = x.astype(BF16)
    return hi, (x - hi.astype(F32)).astype(BF16)


def dot(a, b):
    return jnp.dot(a, b, preferred_element_type=F32)


def kernel(
    num_blk, num_x, num_kv, group,
    q_hbm, kv_hbm, table_hbm, len_hbm, res_hbm, wo_hbm, gain_hbm, wq_hbm,
    both_ref,
    q_v, kv_v, table_v, len_s, res_v, wo_v, gain_v, wq_v,
    qall, code_v, expand, count8, outs, msgf, msg, recv, recvf, hbuf, hsum,
    local_sem, qs_sem, qr_sem, ms_sem, mr_sem, hs_sem, hr_sem,
):
    me = lax.axis_index("blk")
    kv = lax.axis_index("kv")
    num_z = num_blk // (num_x * 2)
    core = lax.rem(me, 2)
    x_at = [lax.rem(me // 2 + k, num_x) * 2 for k in range(num_x)]
    z_at = [lax.rem(me // (num_x * 2) + k, num_z) * (num_x * 2) for k in range(num_z)]
    core_at = [core, 1 - core]

    def peer(k):
        return z_at[k[0]] + x_at[k[1]] + core_at[k[2]]

    def hops(k):
        return min(k[0], num_z - k[0]) + min(k[1], num_x - k[1]) + 0.1 * k[2]

    others = [(a, b, c) for a in range(num_z) for b in range(num_x) for c in range(2)][1:]
    others.sort(key=hops, reverse=True)
    num_req = qall.shape[0]
    blocks = kv_v.shape[0]
    block = kv_v.shape[2]
    width = hsum.shape[1]
    cols = res_v.shape[1]

    pairs = [
        (q_hbm, q_v), (table_hbm, table_v), (len_hbm, len_s), (kv_hbm, kv_v),
        (res_hbm, res_v), (gain_hbm, gain_v), (wo_hbm, wo_v), (wq_hbm, wq_v),
    ]
    loads = [pltpu.make_async_copy(a, b, local_sem.at[i]) for i, (a, b) in enumerate(pairs)]

    sent = pl.ds(0, 6)
    qall[...] = jnp.zeros_like(qall)
    barrier = pltpu.get_barrier_semaphore()

    for k in others:
        pl.semaphore_signal(barrier, inc=1, device_id={"blk": peer(k)}, device_id_type=MESH)
    for k in range(1, num_kv):
        pl.semaphore_signal(
            barrier, inc=1, device_id={"kv": lax.rem(kv + k, num_kv)}, device_id_type=MESH
        )
    for load in loads:
        load.start()

    loads[0].wait()
    mine = rows_of(q_v[...].astype(F32), group, HEAD).astype(BF16)
    qall[me] = mine

    loads[1].wait()
    loads[2].wait()
    max_blocks = table_v.shape[1]
    lane = lax.broadcasted_iota(jnp.int32, (1, 128), 1)
    row_id = lax.broadcasted_iota(jnp.int32, (blocks, 128), 0)
    best = jnp.full((blocks, 128), -1.0, F32)
    first = me * blocks
    for part in range(max_blocks // 128):
        at = lane + part * 128

        def match(i, acc):
            local = table_v[pl.ds(pl.multiple_of(i * 8, 8), 8), part * 128 : (part + 1) * 128] - first
            for c in range(8):
                r = i * 8 + c
                tokens = jnp.clip(len_s[r] - at * block, 0, block)
                code = (tokens + r * 128).astype(F32)
                acc = jnp.where(row_id == local[c : c + 1, :], code, acc)
            return acc

        best = lax.fori_loop(0, num_req // 8, match, best)
    code = jnp.broadcast_to(jnp.max(best, axis=1, keepdims=True), (blocks, 128))
    code_v[...] = code
    code_row = jnp.transpose(code)[:num_req, :].astype(jnp.int32)
    owns = (code_row >> 7) == lax.broadcasted_iota(jnp.int32, (num_req, blocks), 0)

    col_id = lax.broadcasted_iota(jnp.int32, (16, num_req * 8), 1)
    sub = lax.broadcasted_iota(jnp.int32, (16, 128), 0)

    def widen(i, carry):
        a = jnp.broadcast_to(code_v[pl.ds(2 * i, 1), :], (16, 128))
        b = jnp.broadcast_to(code_v[pl.ds(2 * i + 1, 1), :], (16, 128))
        both = jnp.where(sub < 8, a, b).astype(jnp.int32)
        target = (both >> 7) * 8 + (sub & 7)
        wide = jnp.concatenate([target] * (num_req * 8 // 128), axis=1)
        at16 = pl.multiple_of(i * 16, 16)
        expand[pl.ds(at16, 16), :] = jnp.where(col_id == wide, 1.0, 0.0).astype(BF16)
        count8[pl.ds(at16, 16), :] = jnp.where(both >= 0, both & 127, 0)
        return carry

    lax.fori_loop(0, blocks // 2, widen, 0, unroll=4)

    pl.semaphore_wait(barrier, num_blk - 1 + num_kv - 1)

    def send_query(k):
        pltpu.make_async_remote_copy(
            src_ref=qall.at[me, sent], dst_ref=qall.at[me, sent], send_sem=qs_sem, recv_sem=qr_sem,
            device_id={"blk": peer(k)}, device_id_type=MESH,
        ).start()

    for k in others:
        send_query(k)
    loads[3].wait()
    rows63 = pl.ds(0, num_blk - 1)
    pltpu.make_async_copy(qall.at[rows63, sent], qall.at[rows63, sent], qr_sem).wait()

    flat = qall[...].astype(F32).reshape(num_req * 8, HEAD).astype(BF16)
    asked = dot(expand[...], flat).astype(BF16)

    rows = 32
    toks = 4 * block
    r_i = lax.broadcasted_iota(jnp.int32, (rows, toks), 0) // 8
    t_i = lax.broadcasted_iota(jnp.int32, (rows, toks), 1)
    token = jnp.where(t_i // block == r_i, t_i % block, 4096)
    lane8 = lax.broadcasted_iota(jnp.int32, (8, 128), 1)
    scale = HEAD ** (-0.5)
    groups = blocks // 4
    scores = []
    for g in range(groups):
        q = asked[g * rows : (g + 1) * rows, :]
        k = kv_v[g * 4 : (g + 1) * 4, 0].reshape(toks, HEAD)
        scores.append(lax.dot_general(q, k, (((1,), (1,)), ((), ())), preferred_element_type=F32))
    bmax = jnp.zeros((8, 128), F32)
    bsum = jnp.zeros((8, 128), F32)
    weights = []
    for g in range(groups):
        n = count8[g * rows : (g + 1) * rows, :]
        ok = token < jnp.concatenate([n] * (toks // 128), axis=1)
        s = jnp.where(ok, scores[g] * scale, NEG)
        m = jnp.max(s, axis=1, keepdims=True)
        e = jnp.exp(s - m)
        l = jnp.sum(e, axis=1, keepdims=True)
        weights.append(e.astype(BF16))
        for c in range(4):
            here = lane8 == g * 4 + c
            bmax = jnp.where(here, m[c * 8 : (c + 1) * 8], bmax)
            bsum = jnp.where(here, l[c * 8 : (c + 1) * 8], bsum)
    for g in range(groups):
        v = kv_v[g * 4 : (g + 1) * 4, 1].reshape(toks, HEAD)
        outs[g * rows : (g + 1) * rows, :] = dot(weights[g], v)

    lane_r = lax.broadcasted_iota(jnp.int32, (num_req, 128), 1)
    stats = jnp.zeros((num_req, 128), F32)
    for h in range(group):
        high = jnp.where(owns, bmax[h : h + 1, :], NEG)
        top = jnp.max(high, axis=1, keepdims=True).astype(BF16).astype(F32)
        w = jnp.where(owns, jnp.exp(high - top), 0.0)
        total = jnp.sum(w * bsum[h : h + 1, :], axis=1, keepdims=True)
        w_hi, w_lo = split(w)
        o_hi, o_lo = split(outs[pl.ds(h, blocks, stride=8), :])
        acc = dot(w_hi, o_hi) + dot(w_hi, o_lo) + dot(w_lo, o_hi)
        msgf[pl.ds(h, num_req, stride=8), :] = acc
        sum_hi = total.astype(BF16).astype(F32)
        stats = jnp.where(lane_r == h, top, stats)
        stats = jnp.where(lane_r == h + 8, sum_hi, stats)
        stats = jnp.where(lane_r == h + 16, total - sum_hi, stats)
    msgf[pl.ds(group, num_req, stride=8), :] = stats
    msg[...] = msgf[...].reshape(num_req, 8, 128).astype(BF16)
    recv[me] = msg[me]

    for k in others:
        to = peer(k)
        pltpu.make_async_remote_copy(
            src_ref=msg.at[to, sent], dst_ref=recv.at[me, sent], send_sem=ms_sem, recv_sem=mr_sem,
            device_id={"blk": to}, device_id_type=MESH,
        ).start()
    for load in loads[4:]:
        load.wait()
    pltpu.make_async_copy(recv.at[rows63, sent], recv.at[rows63, sent], mr_sem).wait()

    gain = gain_v[...].astype(F32)
    gain = jnp.concatenate([gain[i : i + 1, :] for i in range(width // 128)], axis=1)
    recvf[...] = recv[...].astype(F32).reshape(num_blk * 8, 128)
    stats = recvf[pl.ds(group, num_blk, stride=8), :]
    sums = pltpu.roll(stats, 128 - 8, 1) + pltpu.roll(stats, 128 - 16, 1)
    tops = jnp.where(lane_r < group, stats, 0.0)
    w = jnp.exp(tops - jnp.max(tops, axis=0, keepdims=True))
    total = jnp.sum(w * sums, axis=0, keepdims=True)
    heads = []
    for h in range(group):
        acc = jnp.sum(w[:, h : h + 1] * recvf[pl.ds(h, num_blk, stride=8), :], axis=0, keepdims=True)
        heads.append(acc / total[:, h : h + 1])
    attn = jnp.concatenate(heads, axis=1)
    attn8 = jnp.broadcast_to(attn, (8, group * HEAD)).astype(BF16)
    hbuf[kv] = dot(attn8, wo_v[...])[:1, :]
    own = pl.ds(pl.multiple_of(kv * cols, 128), cols)
    hbuf[kv, :, own] = hbuf[kv, :, own] + res_v[...].astype(F32)

    hops_y = []
    for j in range(1, num_kv):
        hops_y.append(pltpu.make_async_remote_copy(
            src_ref=hbuf.at[kv], dst_ref=hbuf.at[kv], send_sem=hs_sem.at[j - 1], recv_sem=hr_sem.at[j - 1],
            device_id={"kv": lax.rem(kv + j, num_kv)}, device_id_type=MESH,
        ))
    for hop in hops_y:
        hop.start()
    for hop in hops_y:
        hop.wait_recv()

    hidden = hbuf[0]
    for j in range(1, num_kv):
        hidden = hidden + hbuf[j]
    hsum[...] = hidden
    inverse = lax.rsqrt(jnp.sum(hidden * hidden, axis=1, keepdims=True) / width + 1e-05)
    normed = hidden * inverse * gain
    normed8 = jnp.broadcast_to(normed, (8, width)).astype(BF16)
    both_ref[:, :cols] = hsum[:, own].astype(BF16)
    both_ref[:, cols:] = dot(normed8, wq_v[...])[:1, :].astype(BF16)

    for hop in hops_y:
        hop.wait_send()
    pltpu.make_async_copy(qall.at[rows63, sent], qall.at[rows63, sent], qs_sem).wait()
    pltpu.make_async_copy(recv.at[rows63, sent], recv.at[rows63, sent], ms_sem).wait()


def part(both_ref, stream_ref, next_ref):
    cols = stream_ref.shape[1]
    stream_ref[...] = both_ref[:, :cols]
    next_ref[...] = both_ref[:, cols:]


def per_device(num_blk, num_x, num_kv, queries, kv_pool, block_table, lengths, residual, out_weight, norm_gain, qkv_weight):
    group = queries.shape[1] // HEAD
    num_req, max_blocks = block_table.shape
    blocks, _, block, _ = kv_pool.shape
    width = out_weight.shape[1]
    cols = residual.shape[1]
    out_cols = qkv_weight.shape[1]
    anywhere = pl.BlockSpec(memory_space=pl.ANY)
    vmem = pl.BlockSpec(memory_space=pltpu.VMEM)
    dma = pltpu.SemaphoreType.DMA
    both = pl.pallas_call(
        functools.partial(kernel, num_blk, num_x, num_kv, group),
        out_shape=pltpu.VMEM((1, cols + out_cols), BF16),
        in_specs=[anywhere] * 8,
        out_specs=vmem,
        scratch_shapes=[
            pltpu.VMEM(queries.shape, BF16),
            pltpu.VMEM(kv_pool.shape, BF16),
            pltpu.VMEM(block_table.shape, jnp.int32),
            pltpu.SMEM((num_req,), jnp.int32),
            pltpu.VMEM(residual.shape, BF16),
            pltpu.VMEM(out_weight.shape, BF16),
            pltpu.VMEM((width // 128, 128), BF16),
            pltpu.VMEM(qkv_weight.shape, BF16),
            pltpu.VMEM((num_req, 8, HEAD), BF16),
            pltpu.VMEM((blocks, 128), F32),
            pltpu.VMEM((blocks * 8, num_req * 8), BF16),
            pltpu.VMEM((blocks * 8, 128), jnp.int32),
            pltpu.VMEM((blocks * 8, HEAD), F32),
            pltpu.VMEM((num_req * 8, HEAD), F32),
            pltpu.VMEM((num_req, 8, HEAD), BF16),
            pltpu.VMEM((num_blk, 8, HEAD), BF16),
            pltpu.VMEM((num_blk * 8, HEAD), F32),
            pltpu.VMEM((num_kv, 1, width), F32),
            pltpu.VMEM((1, width), F32),
            dma((8,)), dma, dma, dma, dma, dma((num_kv - 1,)), dma((num_kv - 1,)),
        ],
        compiler_params=pltpu.CompilerParams(
            collective_id=0, has_side_effects=True, vmem_limit_bytes=60 * 1024 * 1024
        ),
    )(queries, kv_pool, block_table, lengths, residual, out_weight, norm_gain.reshape(-1, 128), qkv_weight)
    return pl.pallas_call(
        part,
        out_shape=(
            jax.ShapeDtypeStruct((1, cols), BF16),
            jax.ShapeDtypeStruct((1, out_cols), BF16),
        ),
        in_specs=[vmem],
        out_specs=(vmem, vmem),
    )(pltpu.with_memory_space_constraint(both, pltpu.VMEM))


def solution(mesh):
    placed = (
        P("blk", "kv"),
        P("blk", None, None, "kv"),
        P(),
        P(),
        P("blk", "kv"),
        P("kv", None),
        P(),
        P(None, "kv"),
    )
    return jax.shard_map(
        functools.partial(per_device, mesh.shape["blk"], CHIPS_X, mesh.shape["kv"]),
        mesh=mesh,
        in_specs=placed,
        out_specs=(P("blk", "kv"), P("blk", "kv")),
        check_vma=False,
    )
```

```python
import functools

import jax
import jax.numpy as jnp
from jax import lax
from jax.experimental import pallas as pl
from jax.experimental.pallas import tpu as pltpu
from jax.sharding import PartitionSpec as P

HEAD = 128
MESH = pl.DeviceIdType.MESH
F32 = jnp.float32
BF16 = jnp.bfloat16
NEG = -1e30
CHIPS_X = 4


def rows_of(x, count, width):
    rows = [x[:, i * width : (i + 1) * width] for i in range(count)]
    rows.append(jnp.zeros((8 - count, width), x.dtype))
    return jnp.concatenate(rows, axis=0)


def split(x):
    hi = x.astype(BF16)
    return hi, (x - hi.astype(F32)).astype(BF16)


def dot(a, b):
    return jnp.dot(a, b, preferred_element_type=F32)


def kernel(
    num_blk, num_x, num_kv, group,
    q_hbm, kv_hbm, table_hbm, len_hbm, res_hbm, wo_hbm, gain_hbm, wq_hbm,
    both_ref,
    q_v, kv_v, table_v, len_s, res_v, wo_v, gain_v, wq_v,
    qall, code_v, expand, count8, outs, msgf, msg, recv, recvf, hbuf, hsum,
    local_sem, qs_sem, qr_sem, ms_sem, mr_sem, hs_sem, hr_sem,
):
    me = lax.axis_index("blk")
    kv = lax.axis_index("kv")
    num_z = num_blk // (num_x * 2)
    core = lax.rem(me, 2)
    x_at = [lax.rem(me // 2 + k, num_x) * 2 for k in range(num_x)]
    z_at = [lax.rem(me // (num_x * 2) + k, num_z) * (num_x * 2) for k in range(num_z)]
    core_at = [core, 1 - core]

    def peer(k):
        return z_at[k[0]] + x_at[k[1]] + core_at[k[2]]

    def hops(k):
        return min(k[0], num_z - k[0]) + min(k[1], num_x - k[1]) + 0.1 * k[2]

    others = [(a, b, c) for a in range(num_z) for b in range(num_x) for c in range(2)][1:]
    others.sort(key=hops, reverse=True)
    num_req = qall.shape[0]
    blocks = kv_v.shape[0]
    block = kv_v.shape[2]
    width = hsum.shape[1]
    cols = res_v.shape[1]

    pairs = [
        (q_hbm, q_v), (table_hbm, table_v), (len_hbm, len_s), (kv_hbm, kv_v),
        (res_hbm, res_v), (gain_hbm, gain_v), (wo_hbm, wo_v), (wq_hbm, wq_v),
    ]
    loads = [pltpu.make_async_copy(a, b, local_sem.at[i]) for i, (a, b) in enumerate(pairs)]

    sent = pl.ds(0, 6)
    qall[...] = jnp.zeros_like(qall)
    barrier = pltpu.get_barrier_semaphore()

    for k in others:
        pl.semaphore_signal(barrier, inc=1, device_id={"blk": peer(k)}, device_id_type=MESH)
    for k in range(1, num_kv):
        pl.semaphore_signal(
            barrier, inc=1, device_id={"kv": lax.rem(kv + k, num_kv)}, device_id_type=MESH
        )
    for load in loads:
        load.start()

    loads[0].wait()
    mine = rows_of(q_v[...].astype(F32), group, HEAD).astype(BF16)
    qall[me] = mine

    loads[1].wait()
    loads[2].wait()
    max_blocks = table_v.shape[1]
    lane = lax.broadcasted_iota(jnp.int32, (1, 128), 1)
    row_id = lax.broadcasted_iota(jnp.int32, (blocks, 128), 0)
    best = jnp.full((blocks, 128), -1.0, F32)
    first = me * blocks
    for part in range(max_blocks // 128):
        at = lane + part * 128

        def match(i, acc):
            local = table_v[pl.ds(pl.multiple_of(i * 8, 8), 8), part * 128 : (part + 1) * 128] - first
            for c in range(8):
                r = i * 8 + c
                tokens = jnp.clip(len_s[r] - at * block, 0, block)
                code = (tokens + r * 128).astype(F32)
                acc = jnp.where(row_id == local[c : c + 1, :], code, acc)
            return acc

        best = lax.fori_loop(0, num_req // 8, match, best)
    code = jnp.broadcast_to(jnp.max(best, axis=1, keepdims=True), (blocks, 128))
    code_v[...] = code
    code_row = jnp.transpose(code)[:num_req, :].astype(jnp.int32)
    owns = (code_row >> 7) == lax.broadcasted_iota(jnp.int32, (num_req, blocks), 0)

    col_id = lax.broadcasted_iota(jnp.int32, (16, num_req * 8), 1)
    sub = lax.broadcasted_iota(jnp.int32, (16, 128), 0)

    def widen(i, carry):
        a = jnp.broadcast_to(code_v[pl.ds(2 * i, 1), :], (16, 128))
        b = jnp.broadcast_to(code_v[pl.ds(2 * i + 1, 1), :], (16, 128))
        both = jnp.where(sub < 8, a, b).astype(jnp.int32)
        target = (both >> 7) * 8 + (sub & 7)
        wide = jnp.concatenate([target] * (num_req * 8 // 128), axis=1)
        at16 = pl.multiple_of(i * 16, 16)
        expand[pl.ds(at16, 16), :] = jnp.where(col_id == wide, 1.0, 0.0).astype(BF16)
        count8[pl.ds(at16, 16), :] = jnp.where(both >= 0, both & 127, 0)
        return carry

    lax.fori_loop(0, blocks // 2, widen, 0, unroll=4)

    pl.semaphore_wait(barrier, num_blk - 1 + num_kv - 1)

    def send_query(k):
        pltpu.make_async_remote_copy(
            src_ref=qall.at[me, sent], dst_ref=qall.at[me, sent], send_sem=qs_sem, recv_sem=qr_sem,
            device_id={"blk": peer(k)}, device_id_type=MESH,
        ).start()

    for k in others:
        send_query(k)
    loads[3].wait()
    rows63 = pl.ds(0, num_blk - 1)
    pltpu.make_async_copy(qall.at[rows63, sent], qall.at[rows63, sent], qr_sem).wait()

    flat = qall[...].reshape(num_req * 8, HEAD)
    asked = dot(expand[...], flat).astype(BF16)

    rows = 32
    toks = 4 * block
    r_i = lax.broadcasted_iota(jnp.int32, (rows, toks), 0) // 8
    t_i = lax.broadcasted_iota(jnp.int32, (rows, toks), 1)
    token = jnp.where(t_i // block == r_i, t_i % block, 4096)
    lane8 = lax.broadcasted_iota(jnp.int32, (8, 128), 1)
    scale = HEAD ** (-0.5)
    groups = blocks // 4
    scores = []
    for g in range(groups):
        q = asked[g * rows : (g + 1) * rows, :]
        k = kv_v[g * 4 : (g + 1) * 4, 0].reshape(toks, HEAD)
        scores.append(lax.dot_general(q, k, (((1,), (1,)), ((), ())), preferred_element_type=F32))
    bmax = jnp.zeros((8, 128), F32)
    bsum = jnp.zeros((8, 128), F32)
    weights = []
    for g in range(groups):
        n = count8[g * rows : (g + 1) * rows, :]
        ok = token < jnp.concatenate([n] * (toks // 128), axis=1)
        s = jnp.where(ok, scores[g] * scale, NEG)
        m = jnp.max(s, axis=1, keepdims=True)
        e = jnp.exp(s - m)
        l = jnp.sum(e, axis=1, keepdims=True)
        weights.append(e.astype(BF16))
        for c in range(4):
            here = lane8 == g * 4 + c
            bmax = jnp.where(here, m[c * 8 : (c + 1) * 8], bmax)
            bsum = jnp.where(here, l[c * 8 : (c + 1) * 8], bsum)
    for g in range(groups):
        v = kv_v[g * 4 : (g + 1) * 4, 1].reshape(toks, HEAD)
        outs[g * rows : (g + 1) * rows, :] = dot(weights[g], v)

    lane_r = lax.broadcasted_iota(jnp.int32, (num_req, 128), 1)
    stats = jnp.zeros((num_req, 128), F32)
    for h in range(group):
        high = jnp.where(owns, bmax[h : h + 1, :], NEG)
        top = jnp.max(high, axis=1, keepdims=True).astype(BF16).astype(F32)
        w = jnp.where(owns, jnp.exp(high - top), 0.0)
        total = jnp.sum(w * bsum[h : h + 1, :], axis=1, keepdims=True)
        w_hi, w_lo = split(w)
        o_hi, o_lo = split(outs[pl.ds(h, blocks, stride=8), :])
        acc = dot(w_hi, o_hi) + dot(w_hi, o_lo) + dot(w_lo, o_hi)
        msgf[pl.ds(h, num_req, stride=8), :] = acc
        sum_hi = total.astype(BF16).astype(F32)
        stats = jnp.where(lane_r == h, top, stats)
        stats = jnp.where(lane_r == h + 8, sum_hi, stats)
        stats = jnp.where(lane_r == h + 16, total - sum_hi, stats)
    msgf[pl.ds(group, num_req, stride=8), :] = stats
    msg[...] = msgf[...].reshape(num_req, 8, 128).astype(BF16)
    recv[me] = msg[me]

    for k in others:
        to = peer(k)
        pltpu.make_async_remote_copy(
            src_ref=msg.at[to, sent], dst_ref=recv.at[me, sent], send_sem=ms_sem, recv_sem=mr_sem,
            device_id={"blk": to}, device_id_type=MESH,
        ).start()
    for load in loads[4:]:
        load.wait()
    pltpu.make_async_copy(recv.at[rows63, sent], recv.at[rows63, sent], mr_sem).wait()

    gain = gain_v[...].astype(F32)
    gain = jnp.concatenate([gain[i : i + 1, :] for i in range(width // 128)], axis=1)
    recvf[...] = recv[...].astype(F32).reshape(num_blk * 8, 128)
    stats = recvf[pl.ds(group, num_blk, stride=8), :]
    sums = pltpu.roll(stats, 128 - 8, 1) + pltpu.roll(stats, 128 - 16, 1)
    tops = jnp.where(lane_r < group, stats, 0.0)
    w = jnp.exp(tops - jnp.max(tops, axis=0, keepdims=True))
    total = jnp.sum(w * sums, axis=0, keepdims=True)
    heads = []
    for h in range(group):
        acc = jnp.sum(w[:, h : h + 1] * recvf[pl.ds(h, num_blk, stride=8), :], axis=0, keepdims=True)
        heads.append(acc / total[:, h : h + 1])
    attn = jnp.concatenate(heads, axis=1)
    attn8 = jnp.broadcast_to(attn, (8, group * HEAD)).astype(BF16)
    hbuf[kv] = dot(attn8, wo_v[...])[:1, :]
    own = pl.ds(pl.multiple_of(kv * cols, 128), cols)
    hbuf[kv, :, own] = hbuf[kv, :, own] + res_v[...].astype(F32)

    hops_y = []
    for j in sorted(range(1, num_kv), key=lambda j: -min(j, num_kv - j)):
        hops_y.append(pltpu.make_async_remote_copy(
            src_ref=hbuf.at[kv], dst_ref=hbuf.at[kv], send_sem=hs_sem.at[j - 1], recv_sem=hr_sem.at[j - 1],
            device_id={"kv": lax.rem(kv + j, num_kv)}, device_id_type=MESH,
        ))
    for hop in hops_y:
        hop.start()
    for hop in hops_y:
        hop.wait_recv()

    hidden = hbuf[0]
    for j in range(1, num_kv):
        hidden = hidden + hbuf[j]
    hsum[...] = hidden
    inverse = lax.rsqrt(jnp.sum(hidden * hidden, axis=1, keepdims=True) / width + 1e-05)
    normed = hidden * inverse * gain
    normed8 = jnp.broadcast_to(normed, (8, width)).astype(BF16)
    both_ref[:, :cols] = hsum[:, own].astype(BF16)
    both_ref[:, cols:] = dot(normed8, wq_v[...])[:1, :].astype(BF16)

    for hop in hops_y:
        hop.wait_send()
    pltpu.make_async_copy(qall.at[rows63, sent], qall.at[rows63, sent], qs_sem).wait()
    pltpu.make_async_copy(recv.at[rows63, sent], recv.at[rows63, sent], ms_sem).wait()


def part(both_ref, stream_ref, next_ref):
    cols = stream_ref.shape[1]
    stream_ref[...] = both_ref[:, :cols]
    next_ref[...] = both_ref[:, cols:]


def per_device(num_blk, num_x, num_kv, queries, kv_pool, block_table, lengths, residual, out_weight, norm_gain, qkv_weight):
    group = queries.shape[1] // HEAD
    num_req, max_blocks = block_table.shape
    blocks, _, block, _ = kv_pool.shape
    width = out_weight.shape[1]
    cols = residual.shape[1]
    out_cols = qkv_weight.shape[1]
    anywhere = pl.BlockSpec(memory_space=pl.ANY)
    vmem = pl.BlockSpec(memory_space=pltpu.VMEM)
    dma = pltpu.SemaphoreType.DMA
    both = pl.pallas_call(
        functools.partial(kernel, num_blk, num_x, num_kv, group),
        out_shape=pltpu.VMEM((1, cols + out_cols), BF16),
        in_specs=[anywhere] * 8,
        out_specs=vmem,
        scratch_shapes=[
            pltpu.VMEM(queries.shape, BF16),
            pltpu.VMEM(kv_pool.shape, BF16),
            pltpu.VMEM(block_table.shape, jnp.int32),
            pltpu.SMEM((num_req,), jnp.int32),
            pltpu.VMEM(residual.shape, BF16),
            pltpu.VMEM(out_weight.shape, BF16),
            pltpu.VMEM((width // 128, 128), BF16),
            pltpu.VMEM(qkv_weight.shape, BF16),
            pltpu.VMEM((num_req, 8, HEAD), BF16),
            pltpu.VMEM((blocks, 128), F32),
            pltpu.VMEM((blocks * 8, num_req * 8), BF16),
            pltpu.VMEM((blocks * 8, 128), jnp.int32),
            pltpu.VMEM((blocks * 8, HEAD), F32),
            pltpu.VMEM((num_req * 8, HEAD), F32),
            pltpu.VMEM((num_req, 8, HEAD), BF16),
            pltpu.VMEM((num_blk, 8, HEAD), BF16),
            pltpu.VMEM((num_blk * 8, HEAD), F32),
            pltpu.VMEM((num_kv, 1, width), F32),
            pltpu.VMEM((1, width), F32),
            dma((8,)), dma, dma, dma, dma, dma((num_kv - 1,)), dma((num_kv - 1,)),
        ],
        compiler_params=pltpu.CompilerParams(
            collective_id=0, has_side_effects=True, vmem_limit_bytes=60 * 1024 * 1024
        ),
    )(queries, kv_pool, block_table, lengths, residual, out_weight, norm_gain.reshape(-1, 128), qkv_weight)
    return pl.pallas_call(
        part,
        out_shape=(
            jax.ShapeDtypeStruct((1, cols), BF16),
            jax.ShapeDtypeStruct((1, out_cols), BF16),
        ),
        in_specs=[vmem],
        out_specs=(vmem, vmem),
    )(pltpu.with_memory_space_constraint(both, pltpu.VMEM))


def solution(mesh):
    placed = (
        P("blk", "kv"),
        P("blk", None, None, "kv"),
        P(),
        P(),
        P("blk", "kv"),
        P("kv", None),
        P(),
        P(None, "kv"),
    )
    return jax.shard_map(
        functools.partial(per_device, mesh.shape["blk"], CHIPS_X, mesh.shape["kv"]),
        mesh=mesh,
        in_specs=placed,
        out_specs=(P("blk", "kv"), P("blk", "kv")),
        check_vma=False,
    )
```

```python
import functools

import jax
import jax.numpy as jnp
from jax import lax
from jax.experimental import pallas as pl
from jax.experimental.pallas import tpu as pltpu
from jax.sharding import PartitionSpec as P

HEAD = 128
MESH = pl.DeviceIdType.MESH
F32 = jnp.float32
BF16 = jnp.bfloat16
NEG = -1e30
CHIPS_X = 4


def rows_of(x, count, width):
    rows = [x[:, i * width : (i + 1) * width] for i in range(count)]
    rows.append(jnp.zeros((8 - count, width), x.dtype))
    return jnp.concatenate(rows, axis=0)


def split(x):
    hi = x.astype(BF16)
    return hi, (x - hi.astype(F32)).astype(BF16)


def dot(a, b):
    return jnp.dot(a, b, preferred_element_type=F32)


def kernel(
    num_blk, num_x, num_kv, group,
    q_hbm, kv_hbm, table_hbm, len_hbm, res_hbm, wo_hbm, gain_hbm, wq_hbm,
    both_ref,
    q_v, kv_v, table_v, len_s, res_v, wo_v, gain_v, wq_v,
    qall, code_v, expand, count8, outs, msgf, msg, recv, recvf, hbuf, hsum,
    local_sem, qs_sem, qr_sem, ms_sem, mr_sem, hs_sem, hr_sem,
):
    me = lax.axis_index("blk")
    kv = lax.axis_index("kv")
    num_z = num_blk // (num_x * 2)
    core = lax.rem(me, 2)
    x_at = [lax.rem(me // 2 + k, num_x) * 2 for k in range(num_x)]
    z_at = [lax.rem(me // (num_x * 2) + k, num_z) * (num_x * 2) for k in range(num_z)]
    core_at = [core, 1 - core]

    def peer(k):
        return z_at[k[0]] + x_at[k[1]] + core_at[k[2]]

    def hops(k):
        return min(k[0], num_z - k[0]) + min(k[1], num_x - k[1]) + 0.1 * k[2]

    others = [(a, b, c) for a in range(num_z) for b in range(num_x) for c in range(2)][1:]
    others.sort(key=hops, reverse=True)
    num_req = qall.shape[0]
    blocks = kv_v.shape[0]
    block = kv_v.shape[2]
    width = hsum.shape[1]
    cols = res_v.shape[1]

    pairs = [
        (q_hbm, q_v), (table_hbm, table_v), (len_hbm, len_s), (kv_hbm, kv_v),
        (res_hbm, res_v), (gain_hbm, gain_v), (wo_hbm, wo_v), (wq_hbm, wq_v),
    ]
    loads = [pltpu.make_async_copy(a, b, local_sem.at[i]) for i, (a, b) in enumerate(pairs)]

    sent = pl.ds(0, 6)
    qall[...] = jnp.zeros_like(qall)
    barrier = pltpu.get_barrier_semaphore()

    for k in others:
        pl.semaphore_signal(barrier, inc=1, device_id={"blk": peer(k)}, device_id_type=MESH)
    for k in range(1, num_kv):
        pl.semaphore_signal(
            barrier, inc=1, device_id={"kv": lax.rem(kv + k, num_kv)}, device_id_type=MESH
        )
    for load in loads:
        load.start()

    loads[0].wait()
    mine = rows_of(q_v[...].astype(F32), group, HEAD).astype(BF16)
    qall[me] = mine

    loads[1].wait()
    loads[2].wait()
    max_blocks = table_v.shape[1]
    lane = lax.broadcasted_iota(jnp.int32, (1, 128), 1)
    row_id = lax.broadcasted_iota(jnp.int32, (blocks, 128), 0)
    best = jnp.full((blocks, 128), -1.0, F32)
    first = me * blocks
    for part in range(max_blocks // 128):
        at = lane + part * 128

        def match(i, acc):
            local = table_v[pl.ds(pl.multiple_of(i * 8, 8), 8), part * 128 : (part + 1) * 128] - first
            for c in range(8):
                r = i * 8 + c
                tokens = jnp.clip(len_s[r] - at * block, 0, block)
                code = (tokens + r * 128).astype(F32)
                acc = jnp.where(row_id == local[c : c + 1, :], code, acc)
            return acc

        best = lax.fori_loop(0, num_req // 8, match, best)
    code = jnp.broadcast_to(jnp.max(best, axis=1, keepdims=True), (blocks, 128))
    code_v[...] = code
    code_row = jnp.transpose(code)[:num_req, :].astype(jnp.int32)
    owns = (code_row >> 7) == lax.broadcasted_iota(jnp.int32, (num_req, blocks), 0)

    col_id = lax.broadcasted_iota(jnp.int32, (16, num_req * 8), 1)
    sub = lax.broadcasted_iota(jnp.int32, (16, 128), 0)

    def widen(i, carry):
        a = jnp.broadcast_to(code_v[pl.ds(2 * i, 1), :], (16, 128))
        b = jnp.broadcast_to(code_v[pl.ds(2 * i + 1, 1), :], (16, 128))
        both = jnp.where(sub < 8, a, b).astype(jnp.int32)
        target = (both >> 7) * 8 + (sub & 7)
        wide = jnp.concatenate([target] * (num_req * 8 // 128), axis=1)
        at16 = pl.multiple_of(i * 16, 16)
        expand[pl.ds(at16, 16), :] = jnp.where(col_id == wide, 1.0, 0.0).astype(BF16)
        count8[pl.ds(at16, 16), :] = jnp.where(both >= 0, both & 127, 0)
        return carry

    lax.fori_loop(0, blocks // 2, widen, 0, unroll=4)

    pl.semaphore_wait(barrier, num_blk - 1 + num_kv - 1)

    def send_query(k):
        pltpu.make_async_remote_copy(
            src_ref=qall.at[me, sent], dst_ref=qall.at[me, sent], send_sem=qs_sem, recv_sem=qr_sem,
            device_id={"blk": peer(k)}, device_id_type=MESH,
        ).start()

    for k in others:
        send_query(k)
    loads[3].wait()
    rows63 = pl.ds(0, num_blk - 1)
    pltpu.make_async_copy(qall.at[rows63, sent], qall.at[rows63, sent], qr_sem).wait()

    flat = qall[...].astype(F32).reshape(num_req * 8, HEAD).astype(BF16)
    asked = dot(expand[...], flat).astype(BF16)

    rows = 32
    toks = 4 * block
    r_i = lax.broadcasted_iota(jnp.int32, (rows, toks), 0) // 8
    t_i = lax.broadcasted_iota(jnp.int32, (rows, toks), 1)
    token = jnp.where(t_i // block == r_i, t_i % block, 4096)
    lane8 = lax.broadcasted_iota(jnp.int32, (8, 128), 1)
    scale = HEAD ** (-0.5)
    groups = blocks // 4
    scores = []
    for g in range(groups):
        q = asked[g * rows : (g + 1) * rows, :]
        k = kv_v[g * 4 : (g + 1) * 4, 0].reshape(toks, HEAD)
        scores.append(lax.dot_general(q, k, (((1,), (1,)), ((), ())), preferred_element_type=F32))
    bmax = jnp.zeros((8, 128), F32)
    bsum = jnp.zeros((8, 128), F32)
    weights = []
    for g in range(groups):
        n = count8[g * rows : (g + 1) * rows, :]
        ok = token < jnp.concatenate([n] * (toks // 128), axis=1)
        s = jnp.where(ok, scores[g] * scale, NEG)
        m = jnp.max(s, axis=1, keepdims=True)
        e = jnp.exp(s - m)
        l = jnp.sum(e, axis=1, keepdims=True)
        weights.append(e.astype(BF16))
        for c in range(4):
            here = lane8 == g * 4 + c
            bmax = jnp.where(here, m[c * 8 : (c + 1) * 8], bmax)
            bsum = jnp.where(here, l[c * 8 : (c + 1) * 8], bsum)
    for g in range(groups):
        v = kv_v[g * 4 : (g + 1) * 4, 1].reshape(toks, HEAD)
        outs[g * rows : (g + 1) * rows, :] = dot(weights[g], v)

    lane_r = lax.broadcasted_iota(jnp.int32, (num_req, 128), 1)
    stats = jnp.zeros((num_req, 128), F32)
    for h in range(group):
        high = jnp.where(owns, bmax[h : h + 1, :], NEG)
        top = jnp.max(high, axis=1, keepdims=True).astype(BF16).astype(F32)
        w = jnp.where(owns, jnp.exp(high - top), 0.0)
        total = jnp.sum(w * bsum[h : h + 1, :], axis=1, keepdims=True)
        w_hi, w_lo = split(w)
        o_hi, o_lo = split(outs[pl.ds(h, blocks, stride=8), :])
        acc = dot(w_hi, o_hi) + dot(w_hi, o_lo) + dot(w_lo, o_hi)
        msgf[pl.ds(h, num_req, stride=8), :] = acc
        sum_hi = total.astype(BF16).astype(F32)
        stats = jnp.where(lane_r == h, top, stats)
        stats = jnp.where(lane_r == h + 8, sum_hi, stats)
        stats = jnp.where(lane_r == h + 16, total - sum_hi, stats)
    msgf[pl.ds(group, num_req, stride=8), :] = stats
    msg[...] = msgf[...].reshape(num_req, 8, 128).astype(BF16)
    recv[me] = msg[me]

    for k in others:
        to = peer(k)
        pltpu.make_async_remote_copy(
            src_ref=msg.at[to, sent], dst_ref=recv.at[me, sent], send_sem=ms_sem, recv_sem=mr_sem,
            device_id={"blk": to}, device_id_type=MESH,
        ).start()
    for load in loads[4:]:
        load.wait()
    own = pl.ds(pl.multiple_of(kv * cols, 128), cols)
    hsum[...] = jnp.zeros_like(hsum)
    hsum[:, own] = res_v[...].astype(F32)
    pltpu.make_async_copy(recv.at[rows63, sent], recv.at[rows63, sent], mr_sem).wait()

    gain = gain_v[...].astype(F32)
    gain = jnp.concatenate([gain[i : i + 1, :] for i in range(width // 128)], axis=1)
    recvf[...] = recv[...].astype(F32).reshape(num_blk * 8, 128)
    stats = recvf[pl.ds(group, num_blk, stride=8), :]
    sums = pltpu.roll(stats, 128 - 8, 1) + pltpu.roll(stats, 128 - 16, 1)
    tops = jnp.where(lane_r < group, stats, 0.0)
    w = jnp.exp(tops - jnp.max(tops, axis=0, keepdims=True))
    total = jnp.sum(w * sums, axis=0, keepdims=True)
    heads = []
    for h in range(group):
        acc = jnp.sum(w[:, h : h + 1] * recvf[pl.ds(h, num_blk, stride=8), :], axis=0, keepdims=True)
        heads.append(acc / total[:, h : h + 1])
    attn = jnp.concatenate(heads, axis=1)
    attn8 = jnp.broadcast_to(attn, (8, group * HEAD)).astype(BF16)
    hops_y = []
    half = width // 2
    for part in range(2):
        at = pl.ds(part * half, half)
        hbuf[kv, :, at] = dot(attn8, wo_v[:, at])[:1, :] + hsum[:, at]
        for j in range(1, num_kv):
            sem = part * (num_kv - 1) + j - 1
            hops_y.append(pltpu.make_async_remote_copy(
                src_ref=hbuf.at[kv, :, at], dst_ref=hbuf.at[kv, :, at],
                send_sem=hs_sem.at[sem], recv_sem=hr_sem.at[sem],
                device_id={"kv": lax.rem(kv + j, num_kv)}, device_id_type=MESH,
            ))
            hops_y[-1].start()
    for hop in hops_y:
        hop.wait_recv()

    hidden = hbuf[0]
    for j in range(1, num_kv):
        hidden = hidden + hbuf[j]
    hsum[...] = hidden
    inverse = lax.rsqrt(jnp.sum(hidden * hidden, axis=1, keepdims=True) / width + 1e-05)
    normed = hidden * inverse * gain
    normed8 = jnp.broadcast_to(normed, (8, width)).astype(BF16)
    both_ref[:, :cols] = hsum[:, own].astype(BF16)
    both_ref[:, cols:] = dot(normed8, wq_v[...])[:1, :].astype(BF16)

    for hop in hops_y:
        hop.wait_send()
    pltpu.make_async_copy(qall.at[rows63, sent], qall.at[rows63, sent], qs_sem).wait()
    pltpu.make_async_copy(recv.at[rows63, sent], recv.at[rows63, sent], ms_sem).wait()


def part(both_ref, stream_ref, next_ref):
    cols = stream_ref.shape[1]
    stream_ref[...] = both_ref[:, :cols]
    next_ref[...] = both_ref[:, cols:]


def per_device(num_blk, num_x, num_kv, queries, kv_pool, block_table, lengths, residual, out_weight, norm_gain, qkv_weight):
    group = queries.shape[1] // HEAD
    num_req, max_blocks = block_table.shape
    blocks, _, block, _ = kv_pool.shape
    width = out_weight.shape[1]
    cols = residual.shape[1]
    out_cols = qkv_weight.shape[1]
    anywhere = pl.BlockSpec(memory_space=pl.ANY)
    vmem = pl.BlockSpec(memory_space=pltpu.VMEM)
    dma = pltpu.SemaphoreType.DMA
    both = pl.pallas_call(
        functools.partial(kernel, num_blk, num_x, num_kv, group),
        out_shape=pltpu.VMEM((1, cols + out_cols), BF16),
        in_specs=[anywhere] * 8,
        out_specs=vmem,
        scratch_shapes=[
            pltpu.VMEM(queries.shape, BF16),
            pltpu.VMEM(kv_pool.shape, BF16),
            pltpu.VMEM(block_table.shape, jnp.int32),
            pltpu.SMEM((num_req,), jnp.int32),
            pltpu.VMEM(residual.shape, BF16),
            pltpu.VMEM(out_weight.shape, BF16),
            pltpu.VMEM((width // 128, 128), BF16),
            pltpu.VMEM(qkv_weight.shape, BF16),
            pltpu.VMEM((num_req, 8, HEAD), BF16),
            pltpu.VMEM((blocks, 128), F32),
            pltpu.VMEM((blocks * 8, num_req * 8), BF16),
            pltpu.VMEM((blocks * 8, 128), jnp.int32),
            pltpu.VMEM((blocks * 8, HEAD), F32),
            pltpu.VMEM((num_req * 8, HEAD), F32),
            pltpu.VMEM((num_req, 8, HEAD), BF16),
            pltpu.VMEM((num_blk, 8, HEAD), BF16),
            pltpu.VMEM((num_blk * 8, HEAD), F32),
            pltpu.VMEM((num_kv, 1, width), F32),
            pltpu.VMEM((1, width), F32),
            dma((8,)), dma, dma, dma, dma, dma((2 * num_kv - 2,)), dma((2 * num_kv - 2,)),
        ],
        compiler_params=pltpu.CompilerParams(
            collective_id=0, has_side_effects=True, vmem_limit_bytes=60 * 1024 * 1024
        ),
    )(queries, kv_pool, block_table, lengths, residual, out_weight, norm_gain.reshape(-1, 128), qkv_weight)
    return pl.pallas_call(
        part,
        out_shape=(
            jax.ShapeDtypeStruct((1, cols), BF16),
            jax.ShapeDtypeStruct((1, out_cols), BF16),
        ),
        in_specs=[vmem],
        out_specs=(vmem, vmem),
    )(pltpu.with_memory_space_constraint(both, pltpu.VMEM))


def solution(mesh):
    placed = (
        P("blk", "kv"),
        P("blk", None, None, "kv"),
        P(),
        P(),
        P("blk", "kv"),
        P("kv", None),
        P(),
        P(None, "kv"),
    )
    return jax.shard_map(
        functools.partial(per_device, mesh.shape["blk"], CHIPS_X, mesh.shape["kv"]),
        mesh=mesh,
        in_specs=placed,
        out_specs=(P("blk", "kv"), P("blk", "kv")),
        check_vma=False,
    )
```
